128 devices in a mesh: scen: 8 (over y, core), vox: 16 (over x, z).
Axes of the slice: x: 4, y: 4, z: 4, core: 2. Of those that a mesh axis runs over, the one named last changes fastest.
Arguments:
- dose_blocks: float32 [16, 1280, 128, 128], P('scen', 'vox'), may hold values from 0 to 0.046875
- block_map: int32 [1280, 2], P('vox'), may hold values from 0 to 127, as said below
- block_counts: int32 [16], P('vox'), may hold values from 10 to 80, as said below
- target: float32 [262144], P('vox'), may hold values from 0.5 to 15
- fluence_init: float32 [16384], P('vox'), may hold values from 0.5 to 1.5
Outputs:
- fluence: float32 [16384], P('vox')
- weights: float32 [16, 262144], P('scen', 'vox')
The draws below stay inside these ranges and needn't reach their ends.
Inputs may be any that keep to these rules, and one draw needn't show every extreme that they name: `block_map`: column 0 is a row block of the slot's voxel group, 0 to 127; column 1 a beamlet block, 0 to 127; pairs may repeat. `block_counts`: the slots in use are the first ones of their group; some group uses all 80.
All inputs are finite; a program needn't handle non-finite values.
Results may differ from the reference program's by a relative error of at most 0.0003.
Values sent between devices are 32-bit elements; how exact they have to be, the bound alone decides.
A program may use at most 64 MiB of HBM per device.

```python
import jax
import jax.numpy as jnp
from jax import lax

BS = 128
BEAMLETS = 16384
VOX_DEV = 16384
NB = 80
ROUNDS = 2
ITERS = 2
SCEN = 16
VOXELS = 262144
NBLK = 1280
N_VOX = 16


def draw_block_map(key, part):
    first_key, second_key = jax.random.split(jax.random.fold_in(key, 11))
    row_ids = jax.random.randint(first_key, (NB * N_VOX,), 0, VOX_DEV // BS)
    col_ids = jax.random.randint(second_key, (NB * N_VOX,), 0, BEAMLETS // BS)
    row_ids = row_ids.at[0].set(VOX_DEV // BS - 1)
    col_ids = col_ids.at[0].set(BEAMLETS // BS - 1)
    return jnp.stack([row_ids, col_ids], axis=1).astype(jnp.int32)


def draw_block_counts(key, part):
    first_key, second_key = jax.random.split(jax.random.fold_in(key, 23))
    counts = jax.random.randint(first_key, (N_VOX,), max(1, NB // 8), NB // 2 + 1)
    chosen = jax.random.randint(second_key, (), 0, N_VOX)
    counts = jnp.where(jnp.arange(N_VOX) == chosen, NB, counts)
    return counts.astype(jnp.int32)


def draw_target(key, part):
    mapping = draw_block_map(key, part)
    first_rows = mapping[jnp.arange(N_VOX) * NB, 0]
    base_key, plant_key = jax.random.split(jax.random.fold_in(key, 37))
    voxel = jnp.arange(VOXELS)
    group = voxel // VOX_DEV
    local = voxel % VOX_DEV
    planted = (local // BS == first_rows[group]) & (local % BS % 16 == 0)
    drawn = jax.random.uniform(base_key, (VOXELS,), jnp.float32, 0.5, 1.5)
    strength = jax.random.uniform(plant_key, (VOXELS,), jnp.float32, 4.0, 15.0)
    strength = jnp.where(voxel == VOX_DEV - BS, 15.0, strength)
    return jnp.where(planted, strength, drawn).astype(jnp.float32)


def shard_levels(own_key, dims, cuts, least, top_value):
    def one(dim, shards_of):
        steps = jax.random.uniform(jax.random.fold_in(jax.random.fold_in(own_key, 6), dim), (shards_of,), jnp.float32, least / len(cuts), top_value / len(cuts))
        return jnp.repeat(jnp.exp(steps), dims[dim] // shards_of).reshape((-1,) + (1,) * (len(dims) - dim - 1))

    loudness = one(*cuts[0])
    for cut in cuts[1:]:
        loudness = loudness * one(*cut)
    return loudness


def setup_inputs(seed: int = 0) -> dict:
    keys = jax.random.split(jax.random.key(seed), 6)
    return {
        "dose_blocks": jnp.clip(0.046875 * jax.random.uniform(keys[0], (SCEN, NBLK, BS, BS), jnp.float32) ** shard_levels(keys[0], (SCEN, NBLK, BS, BS), ((0, 8), (1, 16)), -0.2, 0.2), 0.0, 0.046875),
        "block_map": draw_block_map(jax.random.fold_in(keys[5], 71), 0),
        "block_counts": draw_block_counts(jax.random.fold_in(keys[5], 71), 0),
        "target": draw_target(jax.random.fold_in(keys[5], 71), 0),
        "fluence_init": jnp.clip(0.5 + 1.0 * jax.random.uniform(keys[4], (BEAMLETS,), jnp.float32) ** shard_levels(keys[4], (BEAMLETS,), ((0, 16),), -0.2, 0.2), 0.5, 1.5),
    }


HIGHEST = lax.Precision.HIGHEST
SHARPNESS = 2.0
STEP_SIZE = 0.5


def reference(dose_blocks, block_map, block_counts, target, fluence_init):
    slots = jnp.arange(NBLK).astype(jnp.int32)
    groups = (slots // NB).astype(jnp.int32)
    usable = ((slots - groups * NB) < block_counts[groups]).astype(jnp.float32)
    row_ids = (groups * (VOX_DEV // BS) + block_map[:, 0]).astype(jnp.int32)
    row_hot = (row_ids[:, None] == jnp.arange(VOXELS // BS).astype(jnp.int32)[None, :]).astype(jnp.float32) * usable[:, None]
    col_hot = (block_map[:, 1][:, None] == jnp.arange(BEAMLETS // BS).astype(jnp.int32)[None, :]).astype(jnp.float32)

    def forward(copies):
        pieces = copies.reshape(SCEN, BEAMLETS // BS, BS)
        picked = jnp.einsum("nb,sbj->snj", col_hot, pieces, precision=HIGHEST)
        products = jnp.einsum("snij,snj->sni", dose_blocks, picked, precision=HIGHEST)
        summed = jnp.einsum("nr,sni->sri", row_hot, products, precision=HIGHEST)
        return summed.reshape(SCEN, VOXELS)

    def backward(weighted):
        pieces = weighted.reshape(SCEN, VOXELS // BS, BS)
        picked = jnp.einsum("nr,sri->sni", row_hot, pieces, precision=HIGHEST)
        products = jnp.einsum("snij,sni->snj", dose_blocks, picked, precision=HIGHEST)
        summed = jnp.einsum("nb,snj->sbj", col_hot, products, precision=HIGHEST)
        return summed.reshape(SCEN, BEAMLETS)

    fluence = fluence_init
    weights = jnp.zeros((SCEN, VOXELS), jnp.float32)
    for outer_round in range(ROUNDS):
        copies = jnp.broadcast_to(fluence[None, :], (SCEN, BEAMLETS))
        for inner_step in range(ITERS):
            dose = forward(copies)
            excess = dose - target[None, :]
            if inner_step == 0:
                weights = jax.nn.softmax(SHARPNESS * excess * excess, axis=0)
            gradient = backward(2.0 * weights * excess)
            copies = jnp.maximum(copies - STEP_SIZE * gradient, 0.0)
        fluence = jnp.mean(copies, axis=0)
    return fluence, weights
```

```python
import functools

import jax
import jax.numpy as jnp
from jax import lax
from jax.experimental import pallas as pl
from jax.experimental.pallas import tpu as pltpu
from jax.sharding import PartitionSpec as P

ROUNDS = 2
SHARPNESS = 2.0
STEP_SIZE = 0.5
F32 = jnp.float32
BF16 = jnp.bfloat16
MESH = pl.DeviceIdType.MESH
UNROLL = 20
LOADS = 8


def split3(x):
    high = x.astype(BF16)
    rest = x - high.astype(F32)
    mid = rest.astype(BF16)
    low = (rest - mid.astype(F32)).astype(BF16)
    return high, mid, low


def mm(a, b):
    return lax.dot_general(a, b, (((1,), (0,)), ((), ())), preferred_element_type=F32)


def mm_nt(a, b):
    return lax.dot_general(a, b, (((1,), (1,)), ((), ())), preferred_element_type=F32)


def iota(shape, dim):
    return lax.broadcasted_iota(jnp.int32, shape, dim)


def vox_partners(nv, v):
    if nv == 16:
        x, z = v // 4, lax.rem(v, 4)
        hops = [(dx, dz) for dx in range(4) for dz in range(4) if dx or dz]
        hops.sort(key=lambda h: -(min(h[0], 4 - h[0]) + min(h[1], 4 - h[1])))
        return [lax.rem(x + dx, 4) * 4 + lax.rem(z + dz, 4) for dx, dz in hops]
    return [lax.rem(v + k, nv) for k in range(1, nv)]


def kernel(
    nv, ns, slots,
    map_ref, count_ref, target_ref, init_ref, dose_ref,
    out_ref, weights_ref,
    stage, fwd_w, bwd_w, left, right, got_left, got_right,
    col_hot, same3, col3, rep3, spare, target_slot, excess_ref, held_w, copies,
    whole, terms, parts, sums, lse_half, lse_parts, lse_all,
    load_sem, vox_send, vox_recv, scen_send, scen_recv, lse_send, lse_recv,
):
    half = slots // 2
    beam_blocks = nv * 8
    v = lax.axis_index("vox")
    s_me = lax.axis_index("scen")
    ny = ns // 2
    y_me, core = s_me // 2, lax.rem(s_me, 2)
    own = pl.ds(pl.multiple_of(v * 8, 8), 8)
    vox_others = vox_partners(nv, v)
    scen_others = [lax.rem(s_me + k, ns) for k in range(1, ns)]
    twin = s_me + 1 - 2 * core
    chips = [lax.rem(y_me + k, ny) * 2 + core for k in range(1, ny)]
    per_load = slots // LOADS

    def load(s, k):
        rows = pl.ds(k * per_load, per_load)
        return pltpu.make_async_copy(
            dose_ref.at[s, rows], stage.at[s, rows], load_sem.at[s, k]
        )

    for s in range(2):
        for k in range(LOADS):
            load(s, k).start()

    barrier = pltpu.get_barrier_semaphore()
    for t in vox_others:
        pl.semaphore_signal(barrier, inc=1, device_id={"vox": t}, device_id_type=MESH)
    for t in scen_others:
        pl.semaphore_signal(barrier, inc=1, device_id={"scen": t}, device_id_type=MESH)

    left[...] = jnp.zeros_like(left)
    right[...] = jnp.zeros_like(right)

    usable = (iota((slots, 128), 0) < count_ref[0]).astype(F32)
    row_hot = (map_ref[:, 0:1] == iota((slots, 128), 1)).astype(F32) * usable
    col_of = (map_ref[:, 1:2] == iota((slots, beam_blocks), 1)).astype(F32)
    eye_row = (iota((128, 128), 0) == iota((128, 128), 1)).astype(BF16)
    eye_col = (iota((beam_blocks, beam_blocks), 0) == iota((beam_blocks, beam_blocks), 1)).astype(BF16)
    row_b, col_b = row_hot.astype(BF16), col_of.astype(BF16)
    col_hot[...] = col_b
    same3[...] = mm_nt(row_b, jnp.concatenate([row_b] * 3, axis=0)).astype(BF16)
    col3[...] = mm_nt(eye_col, jnp.concatenate([col_b] * 3, axis=0)).astype(BF16)
    same = mm_nt(row_b, row_b)
    earlier = jnp.sum(
        jnp.where(iota((slots, slots), 1) < iota((slots, slots), 0), same, 0.0),
        axis=1, keepdims=True,
    )
    rep_b = jnp.where(earlier < 0.5, row_hot, 0.0).astype(BF16)
    picks = mm_nt(eye_row, jnp.concatenate([rep_b] * 3, axis=0))
    rep3[...] = picks.astype(BF16)
    covered = jnp.sum(picks, axis=1, keepdims=True)
    spare[...] = jnp.broadcast_to(jnp.where(covered > 0.5, 0.0, 1.0 / (2 * ns)), (128, 128))
    tgt = mm(row_b, jnp.concatenate(split3(target_ref[...]), axis=1))
    target_slot[...] = (tgt[:, 0:128] + tgt[:, 128:256]) + tgt[:, 256:384]

    pl.semaphore_wait(barrier, len(vox_others) + len(scen_others))

    def vox_copy(src, dst, slot, target):
        return pltpu.make_async_remote_copy(
            src_ref=src, dst_ref=dst, send_sem=vox_send.at[slot], recv_sem=vox_recv.at[slot],
            device_id={"vox": target}, device_id_type=MESH,
        )

    def vox_wait(slot, ref):
        rest = ref.at[pl.ds(0, (nv - 1) * 8)]
        pltpu.make_async_copy(rest, rest, vox_recv.at[slot]).wait()

    def gather_slot(r, s):
        return 2 + 2 * r + s

    def reduce_slot(r, step, s):
        return 6 + 4 * r + 2 * step + s

    whole[0, own, :] = init_ref[...]
    for t in vox_others:
        vox_copy(init_ref, whole.at[0, own], 0, t).start()

    def send_whole(slot, value):
        whole[slot, own, :] = value
        for t in vox_others:
            vox_copy(whole.at[slot, own], whole.at[slot, own], slot, t).start()

    def convert(s, k):
        load(s, k).wait()
        for u in range(per_load):
            n = k * per_load + u
            pair = lax.rem(n, half)
            at = pl.ds(pl.multiple_of((n // half) * 128, 128), 128)
            block = stage[s, n]
            high = block.astype(BF16)
            low = (block - high.astype(F32)).astype(BF16)
            bwd_w[s, pair, at, 0:128] = high
            bwd_w[s, pair, at, 128:256] = low
            fwd_w[s, pair, at, 0:128] = high.T
            fwd_w[s, pair, at, 128:256] = low.T

    for s in range(2):
        lax.fori_loop(0, LOADS, lambda k, c: (convert(s, k), c)[1], 0)

    def stack(s, pieces):
        for q, piece in enumerate(pieces):
            left[s, pl.ds(q, half, stride=8), :] = piece[0:half]
            right[s, pl.ds(q + 3, half, stride=8), :] = piece[half:slots]

    def multiply(s, weights):
        def some(g, carry):
            for u in range(UNROLL):
                p = g * UNROLL + u
                at = pl.ds(pl.multiple_of(p * 8, 8), 8)
                lhs = jnp.concatenate([left[s, at, :], right[s, at, :]], axis=1).astype(BF16)
                got = mm(lhs, weights[s, p])
                got_left[s, at, :] = got[:, 0:128]
                got_right[s, at, :] = got[:, 128:256]
            return carry

        lax.fori_loop(0, half // UNROLL, some, 0)
        halves = []
        for base in (0, 3):
            total = None
            for q in (2, 1, 0):
                at = pl.ds(base + q, half, stride=8)
                term = got_left[s, at, :] + got_right[s, at, :]
                total = term if total is None else total + term
            halves.append(total)
        return jnp.concatenate(split3(jnp.concatenate(halves, axis=0)), axis=0)

    def pick(slot):
        picked = mm(col_hot[...], jnp.concatenate(split3(whole[slot]), axis=1))
        return [picked[:, 128 * q:128 * q + 128] for q in range(3)]

    def forward(s, pieces):
        stack(s, pieces)
        return mm(same3[...], multiply(s, fwd_w)) - target_slot[...]

    def backward(r, step, s, weighted):
        slot = reduce_slot(r, step, s)
        k = slot - 6
        stack(s, [piece.astype(F32) for piece in split3(weighted)])
        terms[k] = mm(col3[...], multiply(s, bwd_w))
        for t in vox_others:
            vox_copy(
                terms.at[k, pl.ds(pl.multiple_of(t * 8, 8), 8)],
                parts.at[k, own], slot, t,
            ).start()
        parts[k, own, :] = terms[k, own, :]

    def descend(r, step, s):
        slot = reduce_slot(r, step, s)
        k = slot - 6
        vox_wait(slot, parts.at[k])
        gradient = parts[k, 0:8, :]
        for j in range(1, nv):
            gradient = gradient + parts[k, 8 * j:8 * j + 8, :]
        moved = jnp.maximum(copies[s] - STEP_SIZE * gradient, 0.0)
        copies[s] = moved
        return moved

    def merge(values):
        peak = functools.reduce(jnp.maximum, values)
        return peak + jnp.log(sum(jnp.exp(value - peak) for value in values))

    mine = pl.ds(pl.multiple_of(core * half, 8), half)
    other = pl.ds(pl.multiple_of((1 - core) * half, 8), half)

    def lse_copy(src, dst, r, k, target):
        return pltpu.make_async_remote_copy(
            src_ref=src, dst_ref=dst, send_sem=lse_send.at[r, k], recv_sem=lse_recv.at[r, k],
            device_id={"scen": target}, device_id_type=MESH,
        )

    def log_totals(r, scores):
        lse_all[2 * r] = merge(scores)
        first = lse_copy(lse_all.at[2 * r, other], lse_half.at[r], r, 0, twin)
        first.start()
        first.wait_recv()
        chip = merge([lse_all[2 * r, mine, :], lse_half[r]])
        spot = pl.ds(pl.multiple_of(y_me * half, 8), half)
        lse_parts[r, spot, :] = chip
        for t in chips:
            lse_copy(lse_parts.at[r, spot], lse_parts.at[r, spot], r, 1, t).start()
        rest = lse_parts.at[r, pl.ds(0, (ny - 1) * half)]
        pltpu.make_async_copy(rest, rest, lse_recv.at[r, 1]).wait()
        lse_all[2 * r + 1, mine, :] = merge(
            [lse_parts[r, half * j:half * j + half, :] for j in range(ny)]
        )
        last = lse_copy(
            lse_all.at[2 * r + 1, mine], lse_all.at[2 * r + 1, mine], r, 2, twin
        )
        last.start()
        last.wait_recv()
        return lse_all[2 * r + 1]

    def scen_copy(r, t):
        return pltpu.make_async_remote_copy(
            src_ref=sums.at[r, s_me], dst_ref=sums.at[r, s_me],
            send_sem=scen_send.at[r], recv_sem=scen_recv.at[r],
            device_id={"scen": t}, device_id_type=MESH,
        )

    for s in range(2):
        copies[s] = init_ref[...]

    for r in range(ROUNDS):
        vox_wait(r, whole.at[r])
        pieces = pick(r)
        scores = []
        for s in range(2):
            excess = forward(s, pieces)
            excess_ref[s] = excess
            scores.append(SHARPNESS * excess * excess)
        totals = log_totals(r, scores)
        for s in range(2):
            excess = excess_ref[s]
            held = jnp.exp(SHARPNESS * excess * excess - totals)
            held_w[s] = held
            backward(r, 0, s, 2.0 * held * excess)
        if r == ROUNDS - 1:
            for s in range(2):
                pieces = jnp.concatenate(split3(held_w[s]), axis=0)
                weights_ref[s] = mm(rep3[...], pieces) + spare[...]
        for s in range(2):
            send_whole(gather_slot(r, s), descend(r, 0, s))
        for s in range(2):
            slot = gather_slot(r, s)
            vox_wait(slot, whole.at[slot])
            excess = forward(s, pick(slot))
            backward(r, 1, s, 2.0 * held_w[s] * excess)
        moved = descend(r, 1, 0)
        sums[r, s_me] = moved + descend(r, 1, 1)
        for t in scen_others:
            scen_copy(r, t).start()
        pltpu.make_async_copy(
            sums.at[r, pl.ds(0, ns - 1)], sums.at[r, pl.ds(0, ns - 1)], scen_recv.at[r]
        ).wait()
        total = sums[r, 0]
        for j in range(1, ns):
            total = total + sums[r, j]
        fluence = total / (2 * ns)
        if r < ROUNDS - 1:
            for s in range(2):
                copies[s] = fluence
            send_whole(r + 1, fluence)
        else:
            out_ref[...] = fluence

    for slot in range(6 + 4 * ROUNDS):
        rest = whole.at[0, pl.ds(0, (nv - 1) * 8)]
        pltpu.make_async_copy(rest, rest, vox_send.at[slot]).wait()
    for r in range(ROUNDS):
        rest = sums.at[r, pl.ds(0, ns - 1)]
        pltpu.make_async_copy(rest, rest, scen_send.at[r]).wait()
        for k, part in ((0, lse_half.at[r]), (1, lse_parts.at[r, pl.ds(0, (ny - 1) * half)]), (2, lse_half.at[r])):
            pltpu.make_async_copy(part, part, lse_send.at[r, k]).wait()


def body(nv, ns, dose_blocks, block_map, block_counts, target, fluence_init):
    _, slots, side, _ = dose_blocks.shape
    half = slots // 2
    rows = target.shape[0] // side
    beam_blocks = nv * 8
    vmem = pl.BlockSpec(memory_space=pltpu.VMEM)
    out, weights = pl.pallas_call(
        functools.partial(kernel, nv, ns, slots),
        out_shape=(
            jax.ShapeDtypeStruct((8, side), F32),
            jax.ShapeDtypeStruct((2, rows, side), F32),
        ),
        in_specs=[vmem, pl.BlockSpec(memory_space=pltpu.SMEM), vmem, vmem, pl.BlockSpec(memory_space=pl.ANY)],
        out_specs=(vmem, vmem),
        scratch_shapes=[
            pltpu.VMEM((2, slots, side, side), F32),
            pltpu.VMEM((2, half, 2 * side, 2 * side), BF16),
            pltpu.VMEM((2, half, 2 * side, 2 * side), BF16),
            pltpu.VMEM((2, 8 * half, side), F32),
            pltpu.VMEM((2, 8 * half, side), F32),
            pltpu.VMEM((2, 8 * half, side), F32),
            pltpu.VMEM((2, 8 * half, side), F32),
            pltpu.VMEM((slots, beam_blocks), BF16),
            pltpu.VMEM((slots, 3 * slots), BF16),
            pltpu.VMEM((beam_blocks, 3 * slots), BF16),
            pltpu.VMEM((rows, 3 * slots), BF16),
            pltpu.VMEM((rows, side), F32),
            pltpu.VMEM((slots, side), F32),
            pltpu.VMEM((2, slots, side), F32),
            pltpu.VMEM((2, slots, side), F32),
            pltpu.VMEM((2, 8, side), F32),
            pltpu.VMEM((6, beam_blocks, side), F32),
            pltpu.VMEM((8, beam_blocks, side), F32),
            pltpu.VMEM((8, beam_blocks, side), F32),
            pltpu.VMEM((ROUNDS, ns, 8, side), F32),
            pltpu.VMEM((ROUNDS, half, side), F32),
            pltpu.VMEM((ROUNDS, ns // 2 * half, side), F32),
            pltpu.VMEM((2 * ROUNDS, slots, side), F32),
            pltpu.SemaphoreType.DMA((2, LOADS)),
            pltpu.SemaphoreType.DMA((14,)),
            pltpu.SemaphoreType.DMA((14,)),
            pltpu.SemaphoreType.DMA((ROUNDS,)),
            pltpu.SemaphoreType.DMA((ROUNDS,)),
            pltpu.SemaphoreType.DMA((ROUNDS, 3)),
            pltpu.SemaphoreType.DMA((ROUNDS, 3)),
        ],
        compiler_params=pltpu.CompilerParams(
            collective_id=0, has_side_effects=True, vmem_limit_bytes=56 * 2**20
        ),
        name="robust_descent",
    )(
        block_map, block_counts, target.reshape(rows, side), fluence_init.reshape(8, side), dose_blocks
    )
    return out.reshape(-1), weights.reshape(2, -1)


def solution(mesh):
    nv, ns = mesh.shape["vox"], mesh.shape["scen"]
    placed = (P("scen", "vox", None, None), P("vox", None), P("vox"), P("vox"), P("vox"))
    return jax.shard_map(
        functools.partial(body, nv, ns),
        mesh=mesh, in_specs=placed, out_specs=(P("vox"), P("scen", "vox")), check_vma=False,
    )
```

```python
import functools

import jax
import jax.numpy as jnp
from jax import lax
from jax.experimental import pallas as pl
from jax.experimental.pallas import tpu as pltpu
from jax.sharding import PartitionSpec as P

ROUNDS = 2
SHARPNESS = 2.0
STEP_SIZE = 0.5
F32 = jnp.float32
BF16 = jnp.bfloat16
MESH = pl.DeviceIdType.MESH
LOADS = 8


def split3(x):
    high = x.astype(BF16)
    rest = x - high.astype(F32)
    mid = rest.astype(BF16)
    low = (rest - mid.astype(F32)).astype(BF16)
    return high, mid, low


def mm(a, b):
    return lax.dot_general(a, b, (((1,), (0,)), ((), ())), preferred_element_type=F32)


def mm_nt(a, b):
    return lax.dot_general(a, b, (((1,), (1,)), ((), ())), preferred_element_type=F32)


def iota(shape, dim):
    return lax.broadcasted_iota(jnp.int32, shape, dim)


def far_first(n):
    return sorted(range(1, n), key=lambda k: -min(k, n - k))


def vox_partners(nv, v):
    if nv == 16:
        x, z = v // 4, lax.rem(v, 4)
        hops = [(dx, dz) for dx in range(4) for dz in range(4) if dx or dz]
        hops.sort(key=lambda h: -(min(h[0], 4 - h[0]) + min(h[1], 4 - h[1])))
        return [lax.rem(x + dx, 4) * 4 + lax.rem(z + dz, 4) for dx, dz in hops]
    return [lax.rem(v + k, nv) for k in range(1, nv)]


def kernel(
    nv, ns, slots,
    map_ref, count_ref, target_ref, init_ref, dose_ref,
    out_ref, weights_ref,
    stage, fwd_w, bwd_w, left, right, got_left, got_right,
    col_hot, same3, col3, rep3, spare, target_slot, held_w, copies,
    whole, terms, parts, terms_both, parts_both, sums, lse_own, lse_twin, lse_parts,
    load_sem, vox_send, vox_recv, scen_send, scen_recv, lse_send, lse_recv,
):
    half = slots // 2
    beam_blocks = nv * 8
    v = lax.axis_index("vox")
    s_me = lax.axis_index("scen")
    ny = ns // 2
    y_me, core = s_me // 2, lax.rem(s_me, 2)
    own = pl.ds(pl.multiple_of(v * 8, 8), 8)
    vox_others = vox_partners(nv, v)
    twin = s_me + 1 - 2 * core
    chips = [lax.rem(y_me + k, ny) * 2 + c for k in far_first(ny) for c in range(2)]
    scen_others = chips + [twin]
    per_load = slots // LOADS

    def load(s, k):
        rows = pl.ds(k * per_load, per_load)
        return pltpu.make_async_copy(
            dose_ref.at[s, rows], stage.at[s, rows], load_sem.at[s, k]
        )

    for s in range(2):
        for k in range(LOADS):
            load(s, k).start()

    barrier = pltpu.get_barrier_semaphore()
    for t in vox_others:
        pl.semaphore_signal(barrier, inc=1, device_id={"vox": t}, device_id_type=MESH)
    for t in scen_others:
        pl.semaphore_signal(barrier, inc=1, device_id={"scen": t}, device_id_type=MESH)

    left[...] = jnp.zeros_like(left)
    right[...] = jnp.zeros_like(right)

    usable = (iota((128, slots), 1) < count_ref[0]).astype(F32)
    row_t = ((map_ref[0:1, :] == iota((128, slots), 0)).astype(F32) * usable).astype(BF16)
    col_t = (map_ref[1:2, :] == iota((beam_blocks, slots), 0)).astype(F32).astype(BF16)
    eye = (iota((slots, slots), 0) == iota((slots, slots), 1)).astype(F32).astype(BF16)
    eye3 = jnp.concatenate([eye] * 3, axis=0)
    row3_t = mm_nt(row_t, eye3).astype(BF16)
    row_hot = mm_nt(eye, row_t)
    row_b = row_hot.astype(BF16)
    col_hot[...] = mm_nt(eye, col_t).astype(BF16)
    same_all = mm(row_b, row3_t)
    same3[...] = same_all.astype(BF16)
    col3[...] = mm_nt(col_t, eye3).astype(BF16)
    place = iota((slots, 3 * slots), 1)
    earlier = jnp.sum(
        jnp.where(place < iota((slots, 3 * slots), 0), same_all, 0.0), axis=1, keepdims=True
    )
    rep_b = jnp.where(earlier < 0.5, row_hot, 0.0).astype(BF16)
    eye_row = (iota((128, 128), 0) == iota((128, 128), 1)).astype(F32).astype(BF16)
    picks = mm_nt(eye_row, jnp.concatenate([rep_b] * 3, axis=0))
    rep3[...] = picks.astype(BF16)
    covered = jnp.sum(picks, axis=1, keepdims=True)
    spare[...] = jnp.broadcast_to(jnp.where(covered > 0.5, 0.0, 1.0 / (2 * ns)), (128, 128))
    tgt = mm(row_b, jnp.concatenate(split3(target_ref[...]), axis=1))
    target_slot[...] = (tgt[:, 0:128] + tgt[:, 128:256]) + tgt[:, 256:384]

    pl.semaphore_wait(barrier, len(vox_others) + len(scen_others))

    def vox_copy(src, dst, slot, target):
        return pltpu.make_async_remote_copy(
            src_ref=src, dst_ref=dst, send_sem=vox_send.at[slot], recv_sem=vox_recv.at[slot],
            device_id={"vox": target}, device_id_type=MESH,
        )

    def vox_wait(slot, ref):
        rest = ref.at[pl.ds(0, (nv - 1) * 8)]
        pltpu.make_async_copy(rest, rest, vox_recv.at[slot]).wait()

    def gather_slot(r, s):
        return 2 + 2 * r + s

    def reduce_slot(r, s):
        return 6 + 3 * r + s

    whole[0, own, :] = init_ref[...]
    for t in vox_others:
        vox_copy(init_ref, whole.at[0, own], 0, t).start()

    def send_whole(slot, value):
        whole[slot, own, :] = value
        for t in vox_others:
            vox_copy(whole.at[slot, own], whole.at[slot, own], slot, t).start()

    def convert(s, k):
        load(s, k).wait()
        for u in range(per_load):
            n = k * per_load + u
            pair = lax.rem(n, half)
            at = pl.ds(pl.multiple_of((n // half) * 128, 128), 128)
            block = stage[s, n]
            high = block.astype(BF16)
            low = (block - high.astype(F32)).astype(BF16)
            bwd_w[s, pair, at, 0:128] = high
            bwd_w[s, pair, at, 128:256] = low
            fwd_w[s, pair, at, 0:128] = high.T
            fwd_w[s, pair, at, 128:256] = low.T

    for s in range(2):
        lax.fori_loop(0, LOADS, lambda k, c: (convert(s, k), c)[1], 0)

    def stack(k, pieces):
        for q, piece in enumerate(pieces):
            left[k, pl.ds(q, half, stride=8), :] = piece[0:half]
            right[k, pl.ds(q + 3, half, stride=8), :] = piece[half:slots]

    def multiply(k, outs, weights):
        for p in range(half):
            at = pl.ds(p * 8, 8)
            lhs = jnp.concatenate([left[k, at, :], right[k, at, :]], axis=1).astype(BF16)
            for out, s in outs:
                got = mm(lhs, weights[s, p])
                got_left[out, at, :] = got[:, 0:128]
                got_right[out, at, :] = got[:, 128:256]

    def collect(k):
        halves = []
        for base in (0, 3):
            total = None
            for q in (2, 1, 0):
                at = pl.ds(base + q, half, stride=8)
                term = got_left[k, at, :] + got_right[k, at, :]
                total = term if total is None else total + term
            halves.append(total)
        return jnp.concatenate(split3(jnp.concatenate(halves, axis=0)), axis=0)

    def pick(slot):
        picked = mm(col_hot[...], jnp.concatenate(split3(whole[slot]), axis=1))
        return [picked[:, 128 * q:128 * q + 128] for q in range(3)]

    def excess_of(k):
        return mm(same3[...], collect(k)) - target_slot[...]

    def push(k, weighted):
        stack(k, [piece.astype(F32) for piece in split3(weighted)])

    def descend(s, gradient):
        moved = jnp.maximum(copies[s] - STEP_SIZE * gradient, 0.0)
        copies[s] = moved
        return moved

    def add_up(terms_of):
        values = [terms_of(j) for j in range(nv)]
        while len(values) > 1:
            values = [a + b for a, b in zip(values[0::2], values[1::2])]
        return values[0]

    def merge(values):
        peak = functools.reduce(jnp.maximum, values)
        return peak + jnp.log(sum(jnp.exp(value - peak) for value in values))

    mine = pl.ds(pl.multiple_of(core * half, 8), half)

    def lse_copy(src, dst, r, k, target):
        return pltpu.make_async_remote_copy(
            src_ref=src, dst_ref=dst, send_sem=lse_send.at[r, k], recv_sem=lse_recv.at[r, k],
            device_id={"scen": target}, device_id_type=MESH,
        )

    def log_totals(r, scores):
        lse_own[r] = merge(scores)
        first = lse_copy(lse_own.at[r], lse_twin.at[r], r, 0, twin)
        first.start()
        first.wait_recv()
        lse_parts[r, y_me] = merge([lse_own[r], lse_twin[r]])
        for t in chips:
            spot = lse_parts.at[r, y_me, mine]
            lse_copy(spot, spot, r, 1, t).start()
        rest = lse_parts.at[r, pl.ds(0, ny - 1)]
        pltpu.make_async_copy(rest, rest, lse_recv.at[r, 1]).wait()
        return merge([lse_parts[r, j] for j in range(ny)])

    def scen_copy(r, t):
        return pltpu.make_async_remote_copy(
            src_ref=sums.at[r, s_me], dst_ref=sums.at[r, s_me],
            send_sem=scen_send.at[r], recv_sem=scen_recv.at[r],
            device_id={"scen": t}, device_id_type=MESH,
        )

    for s in range(2):
        copies[s] = init_ref[...]

    for r in range(ROUNDS):
        vox_wait(r, whole.at[r])
        stack(0, pick(r))
        multiply(0, [(0, 0), (1, 1)], fwd_w)
        excess = [excess_of(s) for s in range(2)]
        scores = [SHARPNESS * value * value for value in excess]
        totals = log_totals(r, scores)
        for s in range(2):
            held = jnp.exp(scores[s] - totals)
            held_w[s] = held
            push(2 + s, 2.0 * held * excess[s])
        for s in range(2):
            slot = reduce_slot(r, s)
            k = 2 * r + s
            multiply(2 + s, [(2 + s, s)], bwd_w)
            terms[k] = mm(col3[...], collect(2 + s))
            for t in vox_others:
                vox_copy(
                    terms.at[k, pl.ds(pl.multiple_of(t * 8, 8), 8)],
                    parts.at[k, own], slot, t,
                ).start()
            parts[k, own, :] = terms[k, own, :]
        if r == ROUNDS - 1:
            for s in range(2):
                pieces = jnp.concatenate(split3(held_w[s]), axis=0)
                weights_ref[pl.ds(s, 128, stride=2), :] = mm(rep3[...], pieces) + spare[...]
        for s in range(2):
            k = 2 * r + s
            vox_wait(reduce_slot(r, s), parts.at[k])
            gradient = add_up(lambda j: parts[k, 8 * j:8 * j + 8, :])
            send_whole(gather_slot(r, s), descend(s, gradient))

        slot = gather_slot(r, 0)
        vox_wait(slot, whole.at[slot])
        stack(0, pick(slot))
        multiply(0, [(0, 0)], fwd_w)
        slot = gather_slot(r, 1)
        vox_wait(slot, whole.at[slot])
        stack(1, pick(slot))
        push(2, 2.0 * held_w[0] * excess_of(0))
        multiply(1, [(1, 1)], fwd_w)
        multiply(2, [(2, 0)], bwd_w)
        push(3, 2.0 * held_w[1] * excess_of(1))
        terms_both[r, :, 0:8, :] = mm(col3[...], collect(2)).reshape(nv, 8, 128)
        multiply(3, [(3, 1)], bwd_w)
        terms_both[r, :, 8:16, :] = mm(col3[...], collect(3)).reshape(nv, 8, 128)
        slot = reduce_slot(r, 2)
        for t in vox_others:
            vox_copy(terms_both.at[r, t], parts_both.at[r, v], slot, t).start()
        parts_both[r, v] = terms_both[r, v]
        rest = parts_both.at[r, pl.ds(0, nv - 1)]
        pltpu.make_async_copy(rest, rest, vox_recv.at[slot]).wait()
        gradient = add_up(lambda j: parts_both[r, j])
        sums[r, s_me] = descend(0, gradient[0:8]) + descend(1, gradient[8:16])
        for t in scen_others:
            scen_copy(r, t).start()
        rest = sums.at[r, pl.ds(0, ns - 1)]
        pltpu.make_async_copy(rest, rest, scen_recv.at[r]).wait()
        total = sums[r, 0]
        for j in range(1, ns):
            total = total + sums[r, j]
        fluence = total / (2 * ns)
        if r < ROUNDS - 1:
            for s in range(2):
                copies[s] = fluence
            send_whole(r + 1, fluence)
        else:
            out_ref[...] = fluence

    for slot in range(6):
        rest = whole.at[0, pl.ds(0, (nv - 1) * 8)]
        pltpu.make_async_copy(rest, rest, vox_send.at[slot]).wait()
    for r in range(ROUNDS):
        for s in range(2):
            rest = whole.at[0, pl.ds(0, (nv - 1) * 8)]
            pltpu.make_async_copy(rest, rest, vox_send.at[reduce_slot(r, s)]).wait()
        rest = parts_both.at[r, pl.ds(0, nv - 1)]
        pltpu.make_async_copy(rest, rest, vox_send.at[reduce_slot(r, 2)]).wait()
        rest = sums.at[r, pl.ds(0, ns - 1)]
        pltpu.make_async_copy(rest, rest, scen_send.at[r]).wait()
        pltpu.make_async_copy(lse_own.at[r], lse_own.at[r], lse_send.at[r, 0]).wait()
        rest = lse_parts.at[r, pl.ds(0, ny - 1)]
        pltpu.make_async_copy(rest, rest, lse_send.at[r, 1]).wait()


def body(nv, ns, dose_blocks, block_map, block_counts, target, fluence_init):
    _, slots, side, _ = dose_blocks.shape
    half = slots // 2
    rows = target.shape[0] // side
    beam_blocks = nv * 8
    vmem = pl.BlockSpec(memory_space=pltpu.VMEM)
    out, weights = pl.pallas_call(
        functools.partial(kernel, nv, ns, slots),
        out_shape=(
            jax.ShapeDtypeStruct((8, side), F32),
            jax.ShapeDtypeStruct((2 * rows, side), F32),
        ),
        in_specs=[vmem, pl.BlockSpec(memory_space=pltpu.SMEM), vmem, vmem, pl.BlockSpec(memory_space=pl.ANY)],
        out_specs=(vmem, vmem),
        scratch_shapes=[
            pltpu.VMEM((2, slots, side, side), F32),
            pltpu.VMEM((2, half, 2 * side, 2 * side), BF16),
            pltpu.VMEM((2, half, 2 * side, 2 * side), BF16),
            pltpu.VMEM((4, 8 * half, side), F32),
            pltpu.VMEM((4, 8 * half, side), F32),
            pltpu.VMEM((4, 8 * half, side), F32),
            pltpu.VMEM((4, 8 * half, side), F32),
            pltpu.VMEM((slots, beam_blocks), BF16),
            pltpu.VMEM((slots, 3 * slots), BF16),
            pltpu.VMEM((beam_blocks, 3 * slots), BF16),
            pltpu.VMEM((rows, 3 * slots), BF16),
            pltpu.VMEM((rows, side), F32),
            pltpu.VMEM((slots, side), F32),
            pltpu.VMEM((2, slots, side), F32),
            pltpu.VMEM((2, 8, side), F32),
            pltpu.VMEM((6, beam_blocks, side), F32),
            pltpu.VMEM((4, beam_blocks, side), F32),
            pltpu.VMEM((4, beam_blocks, side), F32),
            pltpu.VMEM((ROUNDS, nv, 16, side), F32),
            pltpu.VMEM((ROUNDS, nv, 16, side), F32),
            pltpu.VMEM((ROUNDS, ns, 8, side), F32),
            pltpu.VMEM((ROUNDS, slots, side), F32),
            pltpu.VMEM((ROUNDS, slots, side), F32),
            pltpu.VMEM((ROUNDS, ns // 2, slots, side), F32),
            pltpu.SemaphoreType.DMA((2, LOADS)),
            pltpu.SemaphoreType.DMA((12,)),
            pltpu.SemaphoreType.DMA((12,)),
            pltpu.SemaphoreType.DMA((ROUNDS,)),
            pltpu.SemaphoreType.DMA((ROUNDS,)),
            pltpu.SemaphoreType.DMA((ROUNDS, 2)),
            pltpu.SemaphoreType.DMA((ROUNDS, 2)),
        ],
        compiler_params=pltpu.CompilerParams(
            collective_id=0, has_side_effects=True, vmem_limit_bytes=56 * 2**20
        ),
        name="robust_descent",
    )(
        block_map.T, block_counts, target.reshape(rows, side), fluence_init.reshape(8, side), dose_blocks
    )
    weights = weights.reshape(rows, 2, side).transpose(1, 0, 2)
    return out.reshape(-1), weights.reshape(2, -1)


def solution(mesh):
    nv, ns = mesh.shape["vox"], mesh.shape["scen"]
    placed = (P("scen", "vox", None, None), P("vox", None), P("vox"), P("vox"), P("vox"))
    return jax.shard_map(
        functools.partial(body, nv, ns),
        mesh=mesh, in_specs=placed, out_specs=(P("vox"), P("scen", "vox")), check_vma=False,
    )
```

```python
import functools

import jax
import jax.numpy as jnp
from jax import lax
from jax.experimental import pallas as pl
from jax.experimental.pallas import tpu as pltpu
from jax.sharding import PartitionSpec as P

ROUNDS = 2
SHARPNESS = 2.0
STEP_SIZE = 0.5
F32 = jnp.float32
BF16 = jnp.bfloat16
MESH = pl.DeviceIdType.MESH
LOADS = 8


def split3(x):
    high = x.astype(BF16)
    rest = x - high.astype(F32)
    mid = rest.astype(BF16)
    low = (rest - mid.astype(F32)).astype(BF16)
    return high, mid, low


def mm(a, b):
    return lax.dot_general(a, b, (((1,), (0,)), ((), ())), preferred_element_type=F32)


def mm_nt(a, b):
    return lax.dot_general(a, b, (((1,), (1,)), ((), ())), preferred_element_type=F32)


def iota(shape, dim):
    return lax.broadcasted_iota(jnp.int32, shape, dim)


def far_first(n):
    return sorted(range(1, n), key=lambda k: -min(k, n - k))


def vox_partners(nv, v):
    if nv == 16:
        x, z = v // 4, lax.rem(v, 4)
        hops = [(dx, dz) for dx in range(4) for dz in range(4) if dx or dz]
        hops.sort(key=lambda h: -(min(h[0], 4 - h[0]) + min(h[1], 4 - h[1])))
        return [lax.rem(x + dx, 4) * 4 + lax.rem(z + dz, 4) for dx, dz in hops]
    return [lax.rem(v + k, nv) for k in range(1, nv)]


def kernel(
    nv, ns, slots,
    map_hbm, count_hbm, target_hbm, init_hbm, dose_ref,
    out_ref, weights_ref,
    stage, fwd_w, bwd_w, left, right, got_left, got_right,
    col_hot, same3, col3, rep3, spare, target_slot, held_w, copies,
    whole, terms, parts, terms_both, parts_both, sums, lse_own, lse_twin, lse_parts,
    map_ref, count_ref, target_ref, init_ref, small_sem, load_sem, vox_send, vox_recv, scen_send, scen_recv, lse_send, lse_recv,
):
    half = slots // 2
    beam_blocks = nv * 8
    v = lax.axis_index("vox")
    s_me = lax.axis_index("scen")
    ny = ns // 2
    y_me, core = s_me // 2, lax.rem(s_me, 2)
    own = pl.ds(pl.multiple_of(v * 8, 8), 8)
    vox_others = vox_partners(nv, v)
    twin = s_me + 1 - 2 * core
    chips = [lax.rem(y_me + k, ny) * 2 + c for k in far_first(ny) for c in range(2)]
    scen_others = chips + [twin]
    per_load = slots // LOADS

    def load(s, k):
        rows = pl.ds(k * per_load, per_load)
        return pltpu.make_async_copy(
            dose_ref.at[s, rows], stage.at[s, rows], load_sem.at[s, k]
        )

    barrier = pltpu.get_barrier_semaphore()
    for t in vox_others:
        pl.semaphore_signal(barrier, inc=1, device_id={"vox": t}, device_id_type=MESH)
    for t in scen_others:
        pl.semaphore_signal(barrier, inc=1, device_id={"scen": t}, device_id_type=MESH)

    small = [
        pltpu.make_async_copy(src, dst, small_sem.at[k])
        for k, (src, dst) in enumerate((
            (map_hbm, map_ref), (count_hbm, count_ref), (init_hbm, init_ref), (target_hbm, target_ref)
        ))
    ]
    for copy in small:
        copy.start()
    left[...] = jnp.zeros_like(left)
    right[...] = jnp.zeros_like(right)

    for copy in small:
        copy.wait()
    for s in range(2):
        for k in range(LOADS):
            load(s, k).start()

    usable = (iota((128, slots), 1) < count_ref[0]).astype(F32)
    row_t = ((map_ref[0:1, :] == iota((128, slots), 0)).astype(F32) * usable).astype(BF16)
    col_t = (map_ref[1:2, :] == iota((beam_blocks, slots), 0)).astype(F32).astype(BF16)
    eye = (iota((slots, slots), 0) == iota((slots, slots), 1)).astype(F32).astype(BF16)
    eye3 = jnp.concatenate([eye] * 3, axis=0)
    row3_t = mm_nt(row_t, eye3).astype(BF16)
    row_hot = mm_nt(eye, row_t)
    row_b = row_hot.astype(BF16)
    col_hot[...] = mm_nt(eye, col_t).astype(BF16)
    same_all = mm(row_b, row3_t)
    same3[...] = same_all.astype(BF16)
    col3[...] = mm_nt(col_t, eye3).astype(BF16)
    place = iota((slots, 3 * slots), 1)
    earlier = jnp.sum(
        jnp.where(place < iota((slots, 3 * slots), 0), same_all, 0.0), axis=1, keepdims=True
    )
    rep_b = jnp.where(earlier < 0.5, row_hot, 0.0).astype(BF16)
    eye_row = (iota((128, 128), 0) == iota((128, 128), 1)).astype(F32).astype(BF16)
    picks = mm_nt(eye_row, jnp.concatenate([rep_b] * 3, axis=0))
    rep3[...] = picks.astype(BF16)
    covered = jnp.sum(picks, axis=1, keepdims=True)
    spare[...] = jnp.broadcast_to(jnp.where(covered > 0.5, 0.0, 1.0 / (2 * ns)), (128, 128))
    tgt = mm(row_b, jnp.concatenate(split3(target_ref[...]), axis=1))
    target_slot[...] = (tgt[:, 0:128] + tgt[:, 128:256]) + tgt[:, 256:384]

    pl.semaphore_wait(barrier, len(vox_others) + len(scen_others))

    def vox_copy(src, dst, slot, target):
        return pltpu.make_async_remote_copy(
            src_ref=src, dst_ref=dst, send_sem=vox_send.at[slot], recv_sem=vox_recv.at[slot],
            device_id={"vox": target}, device_id_type=MESH,
        )

    def vox_wait(slot, ref):
        rest = ref.at[pl.ds(0, (nv - 1) * 8)]
        pltpu.make_async_copy(rest, rest, vox_recv.at[slot]).wait()

    def gather_slot(r, s):
        return 2 + 2 * r + s

    def reduce_slot(r, s):
        return 6 + 3 * r + s

    whole[0, own, :] = init_ref[...]
    for t in vox_others:
        vox_copy(init_ref, whole.at[0, own], 0, t).start()

    def send_whole(slot, value):
        whole[slot, own, :] = value
        for t in vox_others:
            vox_copy(whole.at[slot, own], whole.at[slot, own], slot, t).start()

    def convert(s, k):
        load(s, k).wait()
        for u in range(per_load):
            n = k * per_load + u
            pair = lax.rem(n, half)
            at = pl.ds(pl.multiple_of((n // half) * 128, 128), 128)
            block = stage[s, n]
            high = block.astype(BF16)
            low = (block - high.astype(F32)).astype(BF16)
            bwd_w[s, pair, at, 0:128] = high
            bwd_w[s, pair, at, 128:256] = low
            fwd_w[s, pair, at, 0:128] = high.T
            fwd_w[s, pair, at, 128:256] = low.T

    for s in range(2):
        lax.fori_loop(0, LOADS, lambda k, c: (convert(s, k), c)[1], 0)

    def stack(k, pieces):
        for q, piece in enumerate(pieces):
            left[k, pl.ds(q, half, stride=8), :] = piece[0:half]
            right[k, pl.ds(q + 3, half, stride=8), :] = piece[half:slots]

    def multiply(k, outs, weights):
        for p in range(half):
            at = pl.ds(p * 8, 8)
            lhs = jnp.concatenate([left[k, at, :], right[k, at, :]], axis=1).astype(BF16)
            for out, s in outs:
                got = mm(lhs, weights[s, p])
                got_left[out, at, :] = got[:, 0:128]
                got_right[out, at, :] = got[:, 128:256]

    def collect(k):
        halves = []
        for base in (0, 3):
            total = None
            for q in (2, 1, 0):
                at = pl.ds(base + q, half, stride=8)
                term = got_left[k, at, :] + got_right[k, at, :]
                total = term if total is None else total + term
            halves.append(total)
        return jnp.concatenate(split3(jnp.concatenate(halves, axis=0)), axis=0)

    def pick(slot):
        picked = mm(col_hot[...], jnp.concatenate(split3(whole[slot]), axis=1))
        return [picked[:, 128 * q:128 * q + 128] for q in range(3)]

    def excess_of(k):
        return mm(same3[...], collect(k)) - target_slot[...]

    def push(k, weighted):
        stack(k, [piece.astype(F32) for piece in split3(weighted)])

    def descend(s, gradient):
        moved = jnp.maximum(copies[s] - STEP_SIZE * gradient, 0.0)
        copies[s] = moved
        return moved

    def add_up(terms_of):
        values = [terms_of(j) for j in range(nv)]
        while len(values) > 1:
            values = [a + b for a, b in zip(values[0::2], values[1::2])]
        return values[0]

    def merge(values):
        peak = functools.reduce(jnp.maximum, values)
        return peak + jnp.log(sum(jnp.exp(value - peak) for value in values))

    mine = pl.ds(pl.multiple_of(core * half, 8), half)

    def lse_copy(src, dst, r, k, target):
        return pltpu.make_async_remote_copy(
            src_ref=src, dst_ref=dst, send_sem=lse_send.at[r, k], recv_sem=lse_recv.at[r, k],
            device_id={"scen": target}, device_id_type=MESH,
        )

    def log_totals(r, scores):
        lse_own[r] = merge(scores)
        first = lse_copy(lse_own.at[r], lse_twin.at[r], r, 0, twin)
        first.start()
        first.wait_recv()
        lse_parts[r, y_me] = merge([lse_own[r], lse_twin[r]])
        for t in chips:
            spot = lse_parts.at[r, y_me, mine]
            lse_copy(spot, spot, r, 1, t).start()
        rest = lse_parts.at[r, pl.ds(0, ny - 1)]
        pltpu.make_async_copy(rest, rest, lse_recv.at[r, 1]).wait()
        return merge([lse_parts[r, j] for j in range(ny)])

    def scen_copy(r, t):
        return pltpu.make_async_remote_copy(
            src_ref=sums.at[r, s_me], dst_ref=sums.at[r, s_me],
            send_sem=scen_send.at[r], recv_sem=scen_recv.at[r],
            device_id={"scen": t}, device_id_type=MESH,
        )

    for s in range(2):
        copies[s] = init_ref[...]

    for r in range(ROUNDS):
        vox_wait(r, whole.at[r])
        stack(0, pick(r))
        multiply(0, [(0, 0), (1, 1)], fwd_w)
        excess = [excess_of(s) for s in range(2)]
        scores = [SHARPNESS * value * value for value in excess]
        totals = log_totals(r, scores)
        for s in range(2):
            held = jnp.exp(scores[s] - totals)
            held_w[s] = held
            push(2 + s, 2.0 * held * excess[s])
        for s in range(2):
            slot = reduce_slot(r, s)
            k = 2 * r + s
            multiply(2 + s, [(2 + s, s)], bwd_w)
            terms[k] = mm(col3[...], collect(2 + s))
            for t in vox_others:
                vox_copy(
                    terms.at[k, pl.ds(pl.multiple_of(t * 8, 8), 8)],
                    parts.at[k, own], slot, t,
                ).start()
            parts[k, own, :] = terms[k, own, :]
        if r == ROUNDS - 1:
            for s in range(2):
                pieces = jnp.concatenate(split3(held_w[s]), axis=0)
                weights_ref[pl.ds(s, 128, stride=2), :] = mm(rep3[...], pieces) + spare[...]
        for s in range(2):
            k = 2 * r + s
            vox_wait(reduce_slot(r, s), parts.at[k])
            gradient = add_up(lambda j: parts[k, 8 * j:8 * j + 8, :])
            send_whole(gather_slot(r, s), descend(s, gradient))

        slot = gather_slot(r, 0)
        vox_wait(slot, whole.at[slot])
        stack(0, pick(slot))
        multiply(0, [(0, 0)], fwd_w)
        slot = gather_slot(r, 1)
        vox_wait(slot, whole.at[slot])
        stack(1, pick(slot))
        push(2, 2.0 * held_w[0] * excess_of(0))
        multiply(1, [(1, 1)], fwd_w)
        multiply(2, [(2, 0)], bwd_w)
        push(3, 2.0 * held_w[1] * excess_of(1))
        terms_both[r, :, 0:8, :] = mm(col3[...], collect(2)).reshape(nv, 8, 128)
        multiply(3, [(3, 1)], bwd_w)
        terms_both[r, :, 8:16, :] = mm(col3[...], collect(3)).reshape(nv, 8, 128)
        slot = reduce_slot(r, 2)
        for t in vox_others:
            vox_copy(terms_both.at[r, t], parts_both.at[r, v], slot, t).start()
        parts_both[r, v] = terms_both[r, v]
        rest = parts_both.at[r, pl.ds(0, nv - 1)]
        pltpu.make_async_copy(rest, rest, vox_recv.at[slot]).wait()
        gradient = add_up(lambda j: parts_both[r, j])
        sums[r, s_me] = descend(0, gradient[0:8]) + descend(1, gradient[8:16])
        for t in scen_others:
            scen_copy(r, t).start()
        rest = sums.at[r, pl.ds(0, ns - 1)]
        pltpu.make_async_copy(rest, rest, scen_recv.at[r]).wait()
        total = sums[r, 0]
        for j in range(1, ns):
            total = total + sums[r, j]
        fluence = total / (2 * ns)
        if r < ROUNDS - 1:
            for s in range(2):
                copies[s] = fluence
            send_whole(r + 1, fluence)
        else:
            out_ref[...] = fluence

    for slot in range(6):
        rest = whole.at[0, pl.ds(0, (nv - 1) * 8)]
        pltpu.make_async_copy(rest, rest, vox_send.at[slot]).wait()
    for r in range(ROUNDS):
        for s in range(2):
            rest = whole.at[0, pl.ds(0, (nv - 1) * 8)]
            pltpu.make_async_copy(rest, rest, vox_send.at[reduce_slot(r, s)]).wait()
        rest = parts_both.at[r, pl.ds(0, nv - 1)]
        pltpu.make_async_copy(rest, rest, vox_send.at[reduce_slot(r, 2)]).wait()
        rest = sums.at[r, pl.ds(0, ns - 1)]
        pltpu.make_async_copy(rest, rest, scen_send.at[r]).wait()
        pltpu.make_async_copy(lse_own.at[r], lse_own.at[r], lse_send.at[r, 0]).wait()
        rest = lse_parts.at[r, pl.ds(0, ny - 1)]
        pltpu.make_async_copy(rest, rest, lse_send.at[r, 1]).wait()


def hand_on(fluence_ref, weights_ref, fluence_out, weights_out):
    fluence_out[...] = fluence_ref[...]
    weights_out[...] = weights_ref[...]


def body(nv, ns, dose_blocks, block_map, block_counts, target, fluence_init):
    _, slots, side, _ = dose_blocks.shape
    half = slots // 2
    rows = target.shape[0] // side
    beam_blocks = nv * 8
    vmem = pl.BlockSpec(memory_space=pltpu.VMEM)
    out, weights = pl.pallas_call(
        functools.partial(kernel, nv, ns, slots),
        out_shape=(
            jax.ShapeDtypeStruct((8, side), F32),
            jax.ShapeDtypeStruct((2 * rows, side), F32),
        ),
        in_specs=[pl.BlockSpec(memory_space=pltpu.HBM)] * 5,
        out_specs=(vmem, vmem),
        scratch_shapes=[
            pltpu.VMEM((2, slots, side, side), F32),
            pltpu.VMEM((2, half, 2 * side, 2 * side), BF16),
            pltpu.VMEM((2, half, 2 * side, 2 * side), BF16),
            pltpu.VMEM((4, 8 * half, side), F32),
            pltpu.VMEM((4, 8 * half, side), F32),
            pltpu.VMEM((4, 8 * half, side), F32),
            pltpu.VMEM((4, 8 * half, side), F32),
            pltpu.VMEM((slots, beam_blocks), BF16),
            pltpu.VMEM((slots, 3 * slots), BF16),
            pltpu.VMEM((beam_blocks, 3 * slots), BF16),
            pltpu.VMEM((rows, 3 * slots), BF16),
            pltpu.VMEM((rows, side), F32),
            pltpu.VMEM((slots, side), F32),
            pltpu.VMEM((2, slots, side), F32),
            pltpu.VMEM((2, 8, side), F32),
            pltpu.VMEM((6, beam_blocks, side), F32),
            pltpu.VMEM((4, beam_blocks, side), F32),
            pltpu.VMEM((4, beam_blocks, side), F32),
            pltpu.VMEM((ROUNDS, nv, 16, side), F32),
            pltpu.VMEM((ROUNDS, nv, 16, side), F32),
            pltpu.VMEM((ROUNDS, ns, 8, side), F32),
            pltpu.VMEM((ROUNDS, slots, side), F32),
            pltpu.VMEM((ROUNDS, slots, side), F32),
            pltpu.VMEM((ROUNDS, ns // 2, slots, side), F32),
            pltpu.VMEM((2, slots), jnp.int32),
            pltpu.SMEM((1,), jnp.int32),
            pltpu.VMEM((rows, side), F32),
            pltpu.VMEM((8, side), F32),
            pltpu.SemaphoreType.DMA((4,)),
            pltpu.SemaphoreType.DMA((2, LOADS)),
            pltpu.SemaphoreType.DMA((12,)),
            pltpu.SemaphoreType.DMA((12,)),
            pltpu.SemaphoreType.DMA((ROUNDS,)),
            pltpu.SemaphoreType.DMA((ROUNDS,)),
            pltpu.SemaphoreType.DMA((ROUNDS, 2)),
            pltpu.SemaphoreType.DMA((ROUNDS, 2)),
        ],
        compiler_params=pltpu.CompilerParams(
            collective_id=0, has_side_effects=True, vmem_limit_bytes=52 * 2**20
        ),
        name="robust_descent",
    )(
        pltpu.with_memory_space_constraint(block_map.T, pltpu.HBM), block_counts, pltpu.with_memory_space_constraint(target.reshape(rows, side), pltpu.HBM), pltpu.with_memory_space_constraint(fluence_init.reshape(8, side), pltpu.HBM), dose_blocks
    )
    out, weights = pl.pallas_call(
        hand_on,
        out_shape=(
            jax.ShapeDtypeStruct((8, side), F32),
            jax.ShapeDtypeStruct((2 * rows, side), F32),
        ),
        in_specs=[vmem, vmem],
        out_specs=(vmem, vmem),
        compiler_params=pltpu.CompilerParams(vmem_limit_bytes=2**20),
        name="hand_on",
    )(out, weights)
    weights = weights.reshape(rows, 2, side).transpose(1, 0, 2)
    return out.reshape(-1), weights.reshape(2, -1)


def solution(mesh):
    nv, ns = mesh.shape["vox"], mesh.shape["scen"]
    placed = (P("scen", "vox", None, None), P("vox", None), P("vox"), P("vox"), P("vox"))
    return jax.shard_map(
        functools.partial(body, nv, ns),
        mesh=mesh, in_specs=placed, out_specs=(P("vox"), P("scen", "vox")), check_vma=False,
    )
```

```python
import functools

import jax
import jax.numpy as jnp
from jax import lax
from jax.experimental import pallas as pl
from jax.experimental.pallas import tpu as pltpu
from jax.sharding import PartitionSpec as P

ROUNDS = 2
SHARPNESS = 2.0
STEP_SIZE = 0.5
F32 = jnp.float32
BF16 = jnp.bfloat16
MESH = pl.DeviceIdType.MESH
LOADS = 5
VECTOR_SLOTS = 16


def split3(x):
    high = x.astype(BF16)
    rest = x - high.astype(F32)
    mid = rest.astype(BF16)
    low = (rest - mid.astype(F32)).astype(BF16)
    return high, mid, low


def mm(a, b):
    return lax.dot_general(a, b, (((1,), (0,)), ((), ())), preferred_element_type=F32)


def mm_nt(a, b):
    return lax.dot_general(a, b, (((1,), (1,)), ((), ())), preferred_element_type=F32)


def iota(shape, dim):
    return lax.broadcasted_iota(jnp.int32, shape, dim)


def far_first(n):
    return sorted(range(1, n), key=lambda k: -min(k, n - k))


def vox_partners(nv, v):
    if nv == 16:
        x, z = v // 4, lax.rem(v, 4)
        hops = [(dx, dz) for dx in range(4) for dz in range(4) if dx or dz]
        hops.sort(key=lambda h: -(min(h[0], 4 - h[0]) + min(h[1], 4 - h[1])))
        return [lax.rem(x + dx, 4) * 4 + lax.rem(z + dz, 4) for dx, dz in hops]
    return [lax.rem(v + k, nv) for k in range(1, nv)]


def kernel(
    nv, ns, slots,
    map_hbm, count_hbm, target_hbm, init_hbm, dose_ref,
    out_ref, weights_ref,
    stage, fwd_w, bwd_w, left, right, got_left, got_right,
    col_hot, same3, col3, rep3, spare, target_slot, held_w, copies,
    row_in, row_out, whole, terms, parts, terms_both, parts_both, sums, lse_own, lse_twin, lse_parts,
    map_ref, count_ref, target_ref, init_ref, small_sem, load_sem, vox_send, vox_recv, scen_send, scen_recv, lse_send, lse_recv,
):
    half = slots // 2
    pairs = (slots - VECTOR_SLOTS) // 2
    beam_blocks = nv * 8
    v = lax.axis_index("vox")
    s_me = lax.axis_index("scen")
    ny = ns // 2
    y_me, core = s_me // 2, lax.rem(s_me, 2)
    own = pl.ds(pl.multiple_of(v * 8, 8), 8)
    vox_others = vox_partners(nv, v)
    twin = s_me + 1 - 2 * core
    chips = [lax.rem(y_me + k, ny) * 2 + c for k in far_first(ny) for c in range(2)]
    scen_others = chips + [twin]
    per_load = slots // LOADS

    def load(s, k):
        rows = pl.ds(k * per_load, per_load)
        return pltpu.make_async_copy(
            dose_ref.at[s, rows], stage.at[s, rows], load_sem.at[s, k]
        )

    barrier = pltpu.get_barrier_semaphore()
    for t in vox_others:
        pl.semaphore_signal(barrier, inc=1, device_id={"vox": t}, device_id_type=MESH)
    for t in scen_others:
        pl.semaphore_signal(barrier, inc=1, device_id={"scen": t}, device_id_type=MESH)

    small = [
        pltpu.make_async_copy(src, dst, small_sem.at[k])
        for k, (src, dst) in enumerate((
            (map_hbm, map_ref), (count_hbm, count_ref), (init_hbm, init_ref), (target_hbm, target_ref)
        ))
    ]
    for copy in small:
        copy.start()
    left[...] = jnp.zeros_like(left)
    right[...] = jnp.zeros_like(right)

    for copy in small:
        copy.wait()
    for s in range(2):
        for k in range(LOADS):
            load(s, k).start()

    usable = (iota((128, slots), 1) < count_ref[0]).astype(F32)
    row_t = ((map_ref[0:1, :] == iota((128, slots), 0)).astype(F32) * usable).astype(BF16)
    col_t = (map_ref[1:2, :] == iota((beam_blocks, slots), 0)).astype(F32).astype(BF16)
    eye = (iota((slots, slots), 0) == iota((slots, slots), 1)).astype(F32).astype(BF16)
    eye3 = jnp.concatenate([eye] * 3, axis=0)
    row3_t = mm_nt(row_t, eye3).astype(BF16)
    row_hot = mm_nt(eye, row_t)
    row_b = row_hot.astype(BF16)
    col_hot[...] = mm_nt(eye, col_t).astype(BF16)
    same_all = mm(row_b, row3_t)
    same3[...] = same_all.astype(BF16)
    col3[...] = mm_nt(col_t, eye3).astype(BF16)
    place = iota((slots, 3 * slots), 1)
    earlier = jnp.sum(
        jnp.where(place < iota((slots, 3 * slots), 0), same_all, 0.0), axis=1, keepdims=True
    )
    rep_b = jnp.where(earlier < 0.5, row_hot, 0.0).astype(BF16)
    eye_row = (iota((128, 128), 0) == iota((128, 128), 1)).astype(F32).astype(BF16)
    picks = mm_nt(eye_row, jnp.concatenate([rep_b] * 3, axis=0))
    rep3[...] = picks.astype(BF16)
    covered = jnp.sum(picks, axis=1, keepdims=True)
    spare[...] = jnp.broadcast_to(jnp.where(covered > 0.5, 0.0, 1.0 / (2 * ns)), (128, 128))
    tgt = mm(row_b, jnp.concatenate(split3(target_ref[...]), axis=1))
    target_slot[...] = (tgt[:, 0:128] + tgt[:, 128:256]) + tgt[:, 256:384]

    pl.semaphore_wait(barrier, len(vox_others) + len(scen_others))

    def vox_copy(src, dst, slot, target):
        return pltpu.make_async_remote_copy(
            src_ref=src, dst_ref=dst, send_sem=vox_send.at[slot], recv_sem=vox_recv.at[slot],
            device_id={"vox": target}, device_id_type=MESH,
        )

    def vox_wait(slot, ref):
        rest = ref.at[pl.ds(0, (nv - 1) * 8)]
        pltpu.make_async_copy(rest, rest, vox_recv.at[slot]).wait()

    def gather_slot(r, s):
        return 2 + 2 * r + s

    def reduce_slot(r, s):
        return 6 + 3 * r + s

    whole[0, own, :] = init_ref[...]
    for t in vox_others:
        vox_copy(init_ref, whole.at[0, own], 0, t).start()

    def send_whole(slot, value):
        whole[slot, own, :] = value
        for t in vox_others:
            vox_copy(whole.at[slot, own], whole.at[slot, own], slot, t).start()

    def convert(s, k):
        load(s, k).wait()
        for u in range(per_load):
            n = k * per_load + u
            pair = lax.rem(n, pairs)
            at = pl.ds(pl.multiple_of((n // pairs) * 128, 128), 128)
            block = stage[s, n]
            high = block.astype(BF16)
            low = (block - high.astype(F32)).astype(BF16)
            bwd_w[s, pair, at, 0:128] = high
            bwd_w[s, pair, at, 128:256] = low
            fwd_w[s, pair, at, 0:128] = high.T
            fwd_w[s, pair, at, 128:256] = low.T

    for s in range(2):
        lax.fori_loop(0, 2 * pairs // per_load, lambda k, c: (convert(s, k), c)[1], 0)
        for k in range(2 * pairs // per_load, LOADS):
            load(s, k).wait()

    def stack(k, pieces):
        for q, piece in enumerate(pieces):
            left[k, pl.ds(q, pairs, stride=8), :] = piece[0:pairs]
            right[k, pl.ds(q + 3, pairs, stride=8), :] = piece[pairs:2 * pairs]

    def tile(k, out, s, p, weights):
        at = pl.ds(p * 8, 8)
        lhs = jnp.concatenate([left[k, at, :], right[k, at, :]], axis=1).astype(BF16)
        got = mm(lhs, weights[s, p])
        got_left[out, at, :] = got[:, 0:128]
        got_right[out, at, :] = got[:, 128:256]

    lane = iota((128, 128), 1)

    def multiply_forward(k, outs):
        tiles = [(out, s, p) for out, s in outs for p in range(pairs)]
        rows = [(out, s, n) for out, s in outs for n in range(VECTOR_SLOTS)]
        done = 0
        sums_t = {out: jnp.zeros((128, 128), F32) for out, s in outs}
        for m, (out, s, p) in enumerate(tiles):
            tile(k, out, s, p, fwd_w)
            while done * len(tiles) < (m + 1) * len(rows):
                out, s, n = rows[done]
                done += 1
                product = stage[s, 2 * pairs + n] * row_in[k, n:n + 1, :]
                dose = jnp.sum(product, axis=1, keepdims=True)
                sums_t[out] = jnp.where(lane == n, dose, sums_t[out])
                if n == VECTOR_SLOTS - 1:
                    row_out[out] = sums_t[out].T[0:VECTOR_SLOTS]

    def multiply_backward(k, s, column):
        n = 0
        for p in range(pairs):
            tile(k, k, s, p, bwd_w)
            while n * pairs < (p + 1) * VECTOR_SLOTS:
                product = stage[s, 2 * pairs + n] * column[:, n:n + 1]
                row_out[k, n:n + 1, :] = jnp.sum(product, axis=0, keepdims=True)
                n += 1

    def collect(k):
        blocks = []
        for base in (0, 3):
            total = None
            for q in (2, 1, 0):
                at = pl.ds(base + q, pairs, stride=8)
                term = got_left[k, at, :] + got_right[k, at, :]
                total = term if total is None else total + term
            blocks.append(total)
        blocks.append(row_out[k])
        return jnp.concatenate(split3(jnp.concatenate(blocks, axis=0)), axis=0)

    def pick(slot):
        picked = mm(col_hot[...], jnp.concatenate(split3(whole[slot]), axis=1))
        return [picked[:, 128 * q:128 * q + 128] for q in range(3)]

    def load_forward(k, pieces):
        stack(k, pieces)
        high, mid, low = (piece[2 * pairs:] for piece in pieces)
        row_in[k] = high + (mid + low)

    def excess_of(k):
        return mm(same3[...], collect(k)) - target_slot[...]

    def load_backward(k, weighted):
        stack(k, [piece.astype(F32) for piece in split3(weighted)])
        rest = weighted[2 * pairs:]
        fill = jnp.zeros((128 - VECTOR_SLOTS, 128), F32)
        return jnp.concatenate([rest, fill], axis=0).T

    def descend(s, gradient):
        moved = jnp.maximum(copies[s] - STEP_SIZE * gradient, 0.0)
        copies[s] = moved
        return moved

    def add_up(terms_of):
        values = [terms_of(j) for j in range(nv)]
        while len(values) > 1:
            values = [a + b for a, b in zip(values[0::2], values[1::2])]
        return values[0]

    def merge(values):
        peak = functools.reduce(jnp.maximum, values)
        return peak + jnp.log(sum(jnp.exp(value - peak) for value in values))

    mine = pl.ds(pl.multiple_of(core * half, 8), half)

    def lse_copy(src, dst, r, k, target):
        return pltpu.make_async_remote_copy(
            src_ref=src, dst_ref=dst, send_sem=lse_send.at[r, k], recv_sem=lse_recv.at[r, k],
            device_id={"scen": target}, device_id_type=MESH,
        )

    def log_totals(r, scores):
        lse_own[r] = merge(scores)
        first = lse_copy(lse_own.at[r], lse_twin.at[r], r, 0, twin)
        first.start()
        first.wait_recv()
        lse_parts[r, y_me] = merge([lse_own[r], lse_twin[r]])
        for t in chips:
            spot = lse_parts.at[r, y_me, mine]
            lse_copy(spot, spot, r, 1, t).start()
        rest = lse_parts.at[r, pl.ds(0, ny - 1)]
        pltpu.make_async_copy(rest, rest, lse_recv.at[r, 1]).wait()
        return merge([lse_parts[r, j] for j in range(ny)])

    def scen_copy(r, t):
        return pltpu.make_async_remote_copy(
            src_ref=sums.at[r, s_me], dst_ref=sums.at[r, s_me],
            send_sem=scen_send.at[r], recv_sem=scen_recv.at[r],
            device_id={"scen": t}, device_id_type=MESH,
        )

    for s in range(2):
        copies[s] = init_ref[...]

    for r in range(ROUNDS):
        vox_wait(r, whole.at[r])
        load_forward(0, pick(r))
        multiply_forward(0, [(0, 0), (1, 1)])
        excess = [excess_of(s) for s in range(2)]
        scores = [SHARPNESS * value * value for value in excess]
        totals = log_totals(r, scores)
        columns = []
        for s in range(2):
            held = jnp.exp(scores[s] - totals)
            held_w[s] = held
            columns.append(load_backward(2 + s, 2.0 * held * excess[s]))
        for s in range(2):
            slot = reduce_slot(r, s)
            k = 2 * r + s
            multiply_backward(2 + s, s, columns[s])
            terms[k] = mm(col3[...], collect(2 + s))
            for t in vox_others:
                vox_copy(
                    terms.at[k, pl.ds(pl.multiple_of(t * 8, 8), 8)],
                    parts.at[k, own], slot, t,
                ).start()
            parts[k, own, :] = terms[k, own, :]
        if r == ROUNDS - 1:
            for s in range(2):
                pieces = jnp.concatenate(split3(held_w[s]), axis=0)
                weights_ref[pl.ds(s, 128, stride=2), :] = mm(rep3[...], pieces) + spare[...]
        for s in range(2):
            k = 2 * r + s
            vox_wait(reduce_slot(r, s), parts.at[k])
            gradient = add_up(lambda j: parts[k, 8 * j:8 * j + 8, :])
            send_whole(gather_slot(r, s), descend(s, gradient))

        slot = gather_slot(r, 0)
        vox_wait(slot, whole.at[slot])
        load_forward(0, pick(slot))
        multiply_forward(0, [(0, 0)])
        slot = gather_slot(r, 1)
        vox_wait(slot, whole.at[slot])
        load_forward(1, pick(slot))
        column = load_backward(2, 2.0 * held_w[0] * excess_of(0))
        multiply_forward(1, [(1, 1)])
        multiply_backward(2, 0, column)
        column = load_backward(3, 2.0 * held_w[1] * excess_of(1))
        terms_both[r, :, 0:8, :] = mm(col3[...], collect(2)).reshape(nv, 8, 128)
        multiply_backward(3, 1, column)
        terms_both[r, :, 8:16, :] = mm(col3[...], collect(3)).reshape(nv, 8, 128)
        slot = reduce_slot(r, 2)
        for t in vox_others:
            vox_copy(terms_both.at[r, t], parts_both.at[r, v], slot, t).start()
        parts_both[r, v] = terms_both[r, v]
        rest = parts_both.at[r, pl.ds(0, nv - 1)]
        pltpu.make_async_copy(rest, rest, vox_recv.at[slot]).wait()
        gradient = add_up(lambda j: parts_both[r, j])
        sums[r, s_me] = descend(0, gradient[0:8]) + descend(1, gradient[8:16])
        for t in scen_others:
            scen_copy(r, t).start()
        rest = sums.at[r, pl.ds(0, ns - 1)]
        pltpu.make_async_copy(rest, rest, scen_recv.at[r]).wait()
        total = sums[r, 0]
        for j in range(1, ns):
            total = total + sums[r, j]
        fluence = total / (2 * ns)
        if r < ROUNDS - 1:
            for s in range(2):
                copies[s] = fluence
            send_whole(r + 1, fluence)
        else:
            out_ref[...] = fluence

    for slot in range(6):
        rest = whole.at[0, pl.ds(0, (nv - 1) * 8)]
        pltpu.make_async_copy(rest, rest, vox_send.at[slot]).wait()
    for r in range(ROUNDS):
        for s in range(2):
            rest = whole.at[0, pl.ds(0, (nv - 1) * 8)]
            pltpu.make_async_copy(rest, rest, vox_send.at[reduce_slot(r, s)]).wait()
        rest = parts_both.at[r, pl.ds(0, nv - 1)]
        pltpu.make_async_copy(rest, rest, vox_send.at[reduce_slot(r, 2)]).wait()
        rest = sums.at[r, pl.ds(0, ns - 1)]
        pltpu.make_async_copy(rest, rest, scen_send.at[r]).wait()
        pltpu.make_async_copy(lse_own.at[r], lse_own.at[r], lse_send.at[r, 0]).wait()
        rest = lse_parts.at[r, pl.ds(0, ny - 1)]
        pltpu.make_async_copy(rest, rest, lse_send.at[r, 1]).wait()


def hand_on(fluence_ref, weights_ref, fluence_out, weights_out):
    fluence_out[...] = fluence_ref[...]
    weights_out[...] = weights_ref[...]


def body(nv, ns, dose_blocks, block_map, block_counts, target, fluence_init):
    _, slots, side, _ = dose_blocks.shape
    pairs = (slots - VECTOR_SLOTS) // 2
    rows = target.shape[0] // side
    beam_blocks = nv * 8
    vmem = pl.BlockSpec(memory_space=pltpu.VMEM)
    out, weights = pl.pallas_call(
        functools.partial(kernel, nv, ns, slots),
        out_shape=(
            jax.ShapeDtypeStruct((8, side), F32),
            jax.ShapeDtypeStruct((2 * rows, side), F32),
        ),
        in_specs=[pl.BlockSpec(memory_space=pltpu.HBM)] * 5,
        out_specs=(vmem, vmem),
        scratch_shapes=[
            pltpu.VMEM((2, slots, side, side), F32),
            pltpu.VMEM((2, pairs, 2 * side, 2 * side), BF16),
            pltpu.VMEM((2, pairs, 2 * side, 2 * side), BF16),
            pltpu.VMEM((4, 8 * pairs, side), F32),
            pltpu.VMEM((4, 8 * pairs, side), F32),
            pltpu.VMEM((4, 8 * pairs, side), F32),
            pltpu.VMEM((4, 8 * pairs, side), F32),
            pltpu.VMEM((slots, beam_blocks), BF16),
            pltpu.VMEM((slots, 3 * slots), BF16),
            pltpu.VMEM((beam_blocks, 3 * slots), BF16),
            pltpu.VMEM((rows, 3 * slots), BF16),
            pltpu.VMEM((rows, side), F32),
            pltpu.VMEM((slots, side), F32),
            pltpu.VMEM((2, slots, side), F32),
            pltpu.VMEM((2, 8, side), F32),
            pltpu.VMEM((4, VECTOR_SLOTS, side), F32),
            pltpu.VMEM((4, VECTOR_SLOTS, side), F32),
            pltpu.VMEM((6, beam_blocks, side), F32),
            pltpu.VMEM((4, beam_blocks, side), F32),
            pltpu.VMEM((4, beam_blocks, side), F32),
            pltpu.VMEM((ROUNDS, nv, 16, side), F32),
            pltpu.VMEM((ROUNDS, nv, 16, side), F32),
            pltpu.VMEM((ROUNDS, ns, 8, side), F32),
            pltpu.VMEM((ROUNDS, slots, side), F32),
            pltpu.VMEM((ROUNDS, slots, side), F32),
            pltpu.VMEM((ROUNDS, ns // 2, slots, side), F32),
            pltpu.VMEM((2, slots), jnp.int32),
            pltpu.SMEM((1,), jnp.int32),
            pltpu.VMEM((rows, side), F32),
            pltpu.VMEM((8, side), F32),
            pltpu.SemaphoreType.DMA((4,)),
            pltpu.SemaphoreType.DMA((2, LOADS)),
            pltpu.SemaphoreType.DMA((12,)),
            pltpu.SemaphoreType.DMA((12,)),
            pltpu.SemaphoreType.DMA((ROUNDS,)),
            pltpu.SemaphoreType.DMA((ROUNDS,)),
            pltpu.SemaphoreType.DMA((ROUNDS, 2)),
            pltpu.SemaphoreType.DMA((ROUNDS, 2)),
        ],
        compiler_params=pltpu.CompilerParams(
            collective_id=0, has_side_effects=True, vmem_limit_bytes=52 * 2**20
        ),
        name="robust_descent",
    )(
        pltpu.with_memory_space_constraint(block_map.T, pltpu.HBM), block_counts, pltpu.with_memory_space_constraint(target.reshape(rows, side), pltpu.HBM), pltpu.with_memory_space_constraint(fluence_init.reshape(8, side), pltpu.HBM), dose_blocks
    )
    out, weights = pl.pallas_call(
        hand_on,
        out_shape=(
            jax.ShapeDtypeStruct((8, side), F32),
            jax.ShapeDtypeStruct((2 * rows, side), F32),
        ),
        in_specs=[vmem, vmem],
        out_specs=(vmem, vmem),
        compiler_params=pltpu.CompilerParams(vmem_limit_bytes=2**20),
        name="hand_on",
    )(out, weights)
    weights = weights.reshape(rows, 2, side).transpose(1, 0, 2)
    return out.reshape(-1), weights.reshape(2, -1)


def solution(mesh):
    nv, ns = mesh.shape["vox"], mesh.shape["scen"]
    placed = (P("scen", "vox", None, None), P("vox", None), P("vox"), P("vox"), P("vox"))
    return jax.shard_map(
        functools.partial(body, nv, ns),
        mesh=mesh, in_specs=placed, out_specs=(P("vox"), P("scen", "vox")), check_vma=False,
    )
```

```python
import functools

import jax
import jax.numpy as jnp
from jax import lax
from jax.experimental import pallas as pl
from jax.experimental.pallas import tpu as pltpu
from jax.sharding import PartitionSpec as P

ROUNDS = 2
SHARPNESS = 2.0
STEP_SIZE = 0.5
F32 = jnp.float32
BF16 = jnp.bfloat16
MESH = pl.DeviceIdType.MESH
LOADS = 4
VECTOR_SLOTS = 24
GROUP = 4


def split3(x):
    high = x.astype(BF16)
    rest = x - high.astype(F32)
    mid = rest.astype(BF16)
    low = (rest - mid.astype(F32)).astype(BF16)
    return high, mid, low


def mm(a, b):
    return lax.dot_general(a, b, (((1,), (0,)), ((), ())), preferred_element_type=F32)


def mm_nt(a, b):
    return lax.dot_general(a, b, (((1,), (1,)), ((), ())), preferred_element_type=F32)


def iota(shape, dim):
    return lax.broadcasted_iota(jnp.int32, shape, dim)


def far_first(n):
    return sorted(range(1, n), key=lambda k: -min(k, n - k))


def vox_partners(nv, v):
    if nv == 16:
        x, z = v // 4, lax.rem(v, 4)
        hops = [(dx, dz) for dx in range(4) for dz in range(4) if dx or dz]
        hops.sort(key=lambda h: -(min(h[0], 4 - h[0]) + min(h[1], 4 - h[1])))
        return [lax.rem(x + dx, 4) * 4 + lax.rem(z + dz, 4) for dx, dz in hops]
    return [lax.rem(v + k, nv) for k in range(1, nv)]


def kernel(
    nv, ns, slots,
    map_hbm, count_hbm, target_hbm, init_hbm, dose_ref,
    out_ref, weights_ref,
    stage, fwd_w, bwd_w, left, right, got_left, got_right,
    col_hot, same3, col3, rep3, spare, target_slot, held_w, copies,
    row_in, row_out, whole, terms, parts, terms_both, parts_both, sums, lse_own, lse_twin, lse_parts,
    map_ref, count_ref, target_ref, init_ref, small_sem, load_sem, vox_send, vox_recv, scen_send, scen_recv, lse_send, lse_recv,
):
    half = slots // 2
    pairs = (slots - VECTOR_SLOTS) // 2
    beam_blocks = nv * 8
    v = lax.axis_index("vox")
    s_me = lax.axis_index("scen")
    ny = ns // 2
    y_me, core = s_me // 2, lax.rem(s_me, 2)
    own = pl.ds(pl.multiple_of(v * 8, 8), 8)
    vox_others = vox_partners(nv, v)
    twin = s_me + 1 - 2 * core
    chips = [lax.rem(y_me + k, ny) * 2 + c for k in far_first(ny) for c in range(2)]
    scen_others = chips + [twin]
    per_load = slots // LOADS

    def load(s, k):
        rows = pl.ds(k * per_load, per_load)
        return pltpu.make_async_copy(
            dose_ref.at[s, rows], stage.at[s, rows], load_sem.at[s, k]
        )

    barrier = pltpu.get_barrier_semaphore()
    for t in vox_others:
        pl.semaphore_signal(barrier, inc=1, device_id={"vox": t}, device_id_type=MESH)
    for t in scen_others:
        pl.semaphore_signal(barrier, inc=1, device_id={"scen": t}, device_id_type=MESH)

    small = [
        pltpu.make_async_copy(src, dst, small_sem.at[k])
        for k, (src, dst) in enumerate((
            (map_hbm, map_ref), (count_hbm, count_ref), (init_hbm, init_ref), (target_hbm, target_ref)
        ))
    ]
    for copy in small:
        copy.start()
    left[...] = jnp.zeros_like(left)
    right[...] = jnp.zeros_like(right)

    for copy in small:
        copy.wait()
    for s in range(2):
        for k in range(LOADS):
            load(s, k).start()

    usable = (iota((128, slots), 1) < count_ref[0]).astype(F32)
    row_t = ((map_ref[0:1, :] == iota((128, slots), 0)).astype(F32) * usable).astype(BF16)
    col_t = (map_ref[1:2, :] == iota((beam_blocks, slots), 0)).astype(F32).astype(BF16)
    eye = (iota((slots, slots), 0) == iota((slots, slots), 1)).astype(F32).astype(BF16)
    eye3 = jnp.concatenate([eye] * 3, axis=0)
    row3_t = mm_nt(row_t, eye3).astype(BF16)
    row_hot = mm_nt(eye, row_t)
    row_b = row_hot.astype(BF16)
    col_hot[...] = mm_nt(eye, col_t).astype(BF16)
    same_all = mm(row_b, row3_t)
    same3[...] = same_all.astype(BF16)
    col3[...] = mm_nt(col_t, eye3).astype(BF16)
    place = iota((slots, 3 * slots), 1)
    earlier = jnp.sum(
        jnp.where(place < iota((slots, 3 * slots), 0), same_all, 0.0), axis=1, keepdims=True
    )
    rep_b = jnp.where(earlier < 0.5, row_hot, 0.0).astype(BF16)
    eye_row = (iota((128, 128), 0) == iota((128, 128), 1)).astype(F32).astype(BF16)
    picks = mm_nt(eye_row, jnp.concatenate([rep_b] * 3, axis=0))
    rep3[...] = picks.astype(BF16)
    covered = jnp.sum(picks, axis=1, keepdims=True)
    spare[...] = jnp.broadcast_to(jnp.where(covered > 0.5, 0.0, 1.0 / (2 * ns)), (128, 128))
    tgt = mm(row_b, jnp.concatenate(split3(target_ref[...]), axis=1))
    target_slot[...] = (tgt[:, 0:128] + tgt[:, 128:256]) + tgt[:, 256:384]

    pl.semaphore_wait(barrier, len(vox_others) + len(scen_others))

    def vox_copy(src, dst, slot, target):
        return pltpu.make_async_remote_copy(
            src_ref=src, dst_ref=dst, send_sem=vox_send.at[slot], recv_sem=vox_recv.at[slot],
            device_id={"vox": target}, device_id_type=MESH,
        )

    def vox_wait(slot, ref):
        rest = ref.at[pl.ds(0, (nv - 1) * 8)]
        pltpu.make_async_copy(rest, rest, vox_recv.at[slot]).wait()

    def gather_slot(r, s):
        return 2 + 2 * r + s

    def reduce_slot(r, s):
        return 6 + 3 * r + s

    whole[0, own, :] = init_ref[...]
    for t in vox_others:
        vox_copy(init_ref, whole.at[0, own], 0, t).start()

    def send_whole(slot, value):
        whole[slot, own, :] = value
        for t in vox_others:
            vox_copy(whole.at[slot, own], whole.at[slot, own], slot, t).start()

    def convert(s, n):
        for u in range(GROUP):
            pair = lax.rem(n + u, half)
            at = pl.ds(pl.multiple_of(((n + u) // half) * 128, 128), 128)
            block = stage[s, n + u]
            high = block.astype(BF16)
            low = (block - high.astype(F32)).astype(BF16)
            bwd_w[s, pair, at, 0:128] = high
            bwd_w[s, pair, at, 128:256] = low
            fwd_w[s, pair, at, 0:128] = high.T
            fwd_w[s, pair, at, 128:256] = low.T

    for s in range(2):
        for k in range(LOADS):
            load(s, k).wait()
            begin = k * per_load
            end = min(begin + per_load, begin // half * half + pairs)
            lax.fori_loop(
                0, (end - begin) // GROUP,
                lambda g, c: (convert(s, begin + g * GROUP), c)[1], 0,
            )

    others = [n for n in range(slots) if n % half >= pairs]

    def stack(k, pieces):
        for q, piece in enumerate(pieces):
            left[k, pl.ds(q, pairs, stride=8), :] = piece[0:pairs]
            right[k, pl.ds(q + 3, pairs, stride=8), :] = piece[half:half + pairs]

    def tile(k, out, s, p, weights):
        at = pl.ds(p * 8, 8)
        lhs = jnp.concatenate([left[k, at, :], right[k, at, :]], axis=1).astype(BF16)
        got = mm(lhs, weights[s, p])
        got_left[out, at, :] = got[:, 0:128]
        got_right[out, at, :] = got[:, 128:256]

    lane = iota((128, 128), 1)

    def multiply_forward(k, outs):
        tiles = [(out, s, p) for out, s in outs for p in range(pairs)]
        rows = [(out, s, n) for out, s in outs for n in others]
        done = 0
        sums_t = {out: jnp.zeros((128, 128), F32) for out, s in outs}
        for m, (out, s, p) in enumerate(tiles):
            tile(k, out, s, p, fwd_w)
            while done * len(tiles) < (m + 1) * len(rows):
                out, s, n = rows[done]
                done += 1
                product = stage[s, n] * row_in[k, n:n + 1, :]
                dose = jnp.sum(product, axis=1, keepdims=True)
                sums_t[out] = jnp.where(lane == n, dose, sums_t[out])
                if n == others[-1]:
                    by_row = sums_t[out].T
                    for base in (0, half):
                        span = slice(base + pairs, base + half)
                        row_out[out, span, :] = by_row[span]

    def multiply_backward(k, s, column):
        done = 0
        for p in range(pairs):
            tile(k, k, s, p, bwd_w)
            while done * pairs < (p + 1) * len(others):
                n = others[done]
                done += 1
                product = stage[s, n] * column[:, n:n + 1]
                row_out[k, n:n + 1, :] = jnp.sum(product, axis=0, keepdims=True)

    def collect(k):
        for row, base in ((0, 0), (half, 3)):
            total = None
            for q in (2, 1, 0):
                at = pl.ds(base + q, pairs, stride=8)
                term = got_left[k, at, :] + got_right[k, at, :]
                total = term if total is None else total + term
            row_out[k, row:row + pairs, :] = total
        return jnp.concatenate(split3(row_out[k]), axis=0)

    def pick(slot):
        picked = mm(col_hot[...], jnp.concatenate(split3(whole[slot]), axis=1))
        return [picked[:, 128 * q:128 * q + 128] for q in range(3)]

    def load_forward(k, pieces):
        stack(k, pieces)
        high, mid, low = pieces
        row_in[k] = high + (mid + low)

    def excess_of(k):
        return mm(same3[...], collect(k)) - target_slot[...]

    def load_backward(k, weighted):
        stack(k, [piece.astype(F32) for piece in split3(weighted)])
        fill = jnp.zeros((128 - slots, 128), F32)
        return jnp.concatenate([weighted, fill], axis=0).T

    def descend(s, gradient):
        moved = jnp.maximum(copies[s] - STEP_SIZE * gradient, 0.0)
        copies[s] = moved
        return moved

    def add_up(terms_of):
        values = [terms_of(j) for j in range(nv)]
        while len(values) > 1:
            values = [a + b for a, b in zip(values[0::2], values[1::2])]
        return values[0]

    def merge(values):
        peak = functools.reduce(jnp.maximum, values)
        return peak + jnp.log(sum(jnp.exp(value - peak) for value in values))

    mine = pl.ds(pl.multiple_of(core * half, 8), half)

    def lse_copy(src, dst, r, k, target):
        return pltpu.make_async_remote_copy(
            src_ref=src, dst_ref=dst, send_sem=lse_send.at[r, k], recv_sem=lse_recv.at[r, k],
            device_id={"scen": target}, device_id_type=MESH,
        )

    def log_totals(r, scores):
        lse_own[r] = merge(scores)
        first = lse_copy(lse_own.at[r], lse_twin.at[r], r, 0, twin)
        first.start()
        first.wait_recv()
        lse_parts[r, y_me] = merge([lse_own[r], lse_twin[r]])
        for t in chips:
            spot = lse_parts.at[r, y_me, mine]
            lse_copy(spot, spot, r, 1, t).start()
        rest = lse_parts.at[r, pl.ds(0, ny - 1)]
        pltpu.make_async_copy(rest, rest, lse_recv.at[r, 1]).wait()
        return merge([lse_parts[r, j] for j in range(ny)])

    def scen_copy(r, t):
        return pltpu.make_async_remote_copy(
            src_ref=sums.at[r, s_me], dst_ref=sums.at[r, s_me],
            send_sem=scen_send.at[r], recv_sem=scen_recv.at[r],
            device_id={"scen": t}, device_id_type=MESH,
        )

    for s in range(2):
        copies[s] = init_ref[...]

    for r in range(ROUNDS):
        vox_wait(r, whole.at[r])
        load_forward(0, pick(r))
        multiply_forward(0, [(0, 0), (1, 1)])
        excess = [excess_of(s) for s in range(2)]
        scores = [SHARPNESS * value * value for value in excess]
        totals = log_totals(r, scores)
        columns = []
        for s in range(2):
            held = jnp.exp(scores[s] - totals)
            held_w[s] = held
            columns.append(load_backward(2 + s, 2.0 * held * excess[s]))
        for s in range(2):
            slot = reduce_slot(r, s)
            k = 2 * r + s
            multiply_backward(2 + s, s, columns[s])
            terms[k] = mm(col3[...], collect(2 + s))
            for t in vox_others:
                vox_copy(
                    terms.at[k, pl.ds(pl.multiple_of(t * 8, 8), 8)],
                    parts.at[k, own], slot, t,
                ).start()
            parts[k, own, :] = terms[k, own, :]
        if r == ROUNDS - 1:
            for s in range(2):
                pieces = jnp.concatenate(split3(held_w[s]), axis=0)
                weights_ref[pl.ds(s, 128, stride=2), :] = mm(rep3[...], pieces) + spare[...]
        for s in range(2):
            k = 2 * r + s
            vox_wait(reduce_slot(r, s), parts.at[k])
            gradient = add_up(lambda j: parts[k, 8 * j:8 * j + 8, :])
            send_whole(gather_slot(r, s), descend(s, gradient))

        slot = gather_slot(r, 0)
        vox_wait(slot, whole.at[slot])
        load_forward(0, pick(slot))
        multiply_forward(0, [(0, 0)])
        slot = gather_slot(r, 1)
        vox_wait(slot, whole.at[slot])
        load_forward(1, pick(slot))
        column = load_backward(2, 2.0 * held_w[0] * excess_of(0))
        multiply_forward(1, [(1, 1)])
        multiply_backward(2, 0, column)
        column = load_backward(3, 2.0 * held_w[1] * excess_of(1))
        terms_both[r, :, 0:8, :] = mm(col3[...], collect(2)).reshape(nv, 8, 128)
        multiply_backward(3, 1, column)
        terms_both[r, :, 8:16, :] = mm(col3[...], collect(3)).reshape(nv, 8, 128)
        slot = reduce_slot(r, 2)
        for t in vox_others:
            vox_copy(terms_both.at[r, t], parts_both.at[r, v], slot, t).start()
        parts_both[r, v] = terms_both[r, v]
        rest = parts_both.at[r, pl.ds(0, nv - 1)]
        pltpu.make_async_copy(rest, rest, vox_recv.at[slot]).wait()
        gradient = add_up(lambda j: parts_both[r, j])
        sums[r, s_me] = descend(0, gradient[0:8]) + descend(1, gradient[8:16])
        for t in scen_others:
            scen_copy(r, t).start()
        rest = sums.at[r, pl.ds(0, ns - 1)]
        pltpu.make_async_copy(rest, rest, scen_recv.at[r]).wait()
        total = sums[r, 0]
        for j in range(1, ns):
            total = total + sums[r, j]
        fluence = total / (2 * ns)
        if r < ROUNDS - 1:
            for s in range(2):
                copies[s] = fluence
            send_whole(r + 1, fluence)
        else:
            out_ref[...] = fluence

    for slot in range(6):
        rest = whole.at[0, pl.ds(0, (nv - 1) * 8)]
        pltpu.make_async_copy(rest, rest, vox_send.at[slot]).wait()
    for r in range(ROUNDS):
        for s in range(2):
            rest = whole.at[0, pl.ds(0, (nv - 1) * 8)]
            pltpu.make_async_copy(rest, rest, vox_send.at[reduce_slot(r, s)]).wait()
        rest = parts_both.at[r, pl.ds(0, nv - 1)]
        pltpu.make_async_copy(rest, rest, vox_send.at[reduce_slot(r, 2)]).wait()
        rest = sums.at[r, pl.ds(0, ns - 1)]
        pltpu.make_async_copy(rest, rest, scen_send.at[r]).wait()
        pltpu.make_async_copy(lse_own.at[r], lse_own.at[r], lse_send.at[r, 0]).wait()
        rest = lse_parts.at[r, pl.ds(0, ny - 1)]
        pltpu.make_async_copy(rest, rest, lse_send.at[r, 1]).wait()


def hand_on(fluence_ref, weights_ref, fluence_out, weights_out):
    fluence_out[...] = fluence_ref[...]
    weights_out[...] = weights_ref[...]


def body(nv, ns, dose_blocks, block_map, block_counts, target, fluence_init):
    _, slots, side, _ = dose_blocks.shape
    pairs = (slots - VECTOR_SLOTS) // 2
    rows = target.shape[0] // side
    beam_blocks = nv * 8
    vmem = pl.BlockSpec(memory_space=pltpu.VMEM)
    out, weights = pl.pallas_call(
        functools.partial(kernel, nv, ns, slots),
        out_shape=(
            jax.ShapeDtypeStruct((8, side), F32),
            jax.ShapeDtypeStruct((2 * rows, side), F32),
        ),
        in_specs=[pl.BlockSpec(memory_space=pltpu.HBM)] * 5,
        out_specs=(vmem, vmem),
        scratch_shapes=[
            pltpu.VMEM((2, slots, side, side), F32),
            pltpu.VMEM((2, pairs, 2 * side, 2 * side), BF16),
            pltpu.VMEM((2, pairs, 2 * side, 2 * side), BF16),
            pltpu.VMEM((4, 8 * pairs, side), F32),
            pltpu.VMEM((4, 8 * pairs, side), F32),
            pltpu.VMEM((4, 8 * pairs, side), F32),
            pltpu.VMEM((4, 8 * pairs, side), F32),
            pltpu.VMEM((slots, beam_blocks), BF16),
            pltpu.VMEM((slots, 3 * slots), BF16),
            pltpu.VMEM((beam_blocks, 3 * slots), BF16),
            pltpu.VMEM((rows, 3 * slots), BF16),
            pltpu.VMEM((rows, side), F32),
            pltpu.VMEM((slots, side), F32),
            pltpu.VMEM((2, slots, side), F32),
            pltpu.VMEM((2, 8, side), F32),
            pltpu.VMEM((4, slots, side), F32),
            pltpu.VMEM((4, slots, side), F32),
            pltpu.VMEM((6, beam_blocks, side), F32),
            pltpu.VMEM((4, beam_blocks, side), F32),
            pltpu.VMEM((4, beam_blocks, side), F32),
            pltpu.VMEM((ROUNDS, nv, 16, side), F32),
            pltpu.VMEM((ROUNDS, nv, 16, side), F32),
            pltpu.VMEM((ROUNDS, ns, 8, side), F32),
            pltpu.VMEM((ROUNDS, slots, side), F32),
            pltpu.VMEM((ROUNDS, slots, side), F32),
            pltpu.VMEM((ROUNDS, ns // 2, slots, side), F32),
            pltpu.VMEM((2, slots), jnp.int32),
            pltpu.SMEM((1,), jnp.int32),
            pltpu.VMEM((rows, side), F32),
            pltpu.VMEM((8, side), F32),
            pltpu.SemaphoreType.DMA((4,)),
            pltpu.SemaphoreType.DMA((2, LOADS)),
            pltpu.SemaphoreType.DMA((12,)),
            pltpu.SemaphoreType.DMA((12,)),
            pltpu.SemaphoreType.DMA((ROUNDS,)),
            pltpu.SemaphoreType.DMA((ROUNDS,)),
            pltpu.SemaphoreType.DMA((ROUNDS, 2)),
            pltpu.SemaphoreType.DMA((ROUNDS, 2)),
        ],
        compiler_params=pltpu.CompilerParams(
            collective_id=0, has_side_effects=True, vmem_limit_bytes=52 * 2**20
        ),
        name="robust_descent",
    )(
        pltpu.with_memory_space_constraint(block_map.T, pltpu.HBM), block_counts, pltpu.with_memory_space_constraint(target.reshape(rows, side), pltpu.HBM), pltpu.with_memory_space_constraint(fluence_init.reshape(8, side), pltpu.HBM), dose_blocks
    )
    out, weights = pl.pallas_call(
        hand_on,
        out_shape=(
            jax.ShapeDtypeStruct((8, side), F32),
            jax.ShapeDtypeStruct((2 * rows, side), F32),
        ),
        in_specs=[vmem, vmem],
        out_specs=(vmem, vmem),
        compiler_params=pltpu.CompilerParams(vmem_limit_bytes=2**20),
        name="hand_on",
    )(out, weights)
    weights = weights.reshape(rows, 2, side).transpose(1, 0, 2)
    return out.reshape(-1), weights.reshape(2, -1)


def solution(mesh):
    nv, ns = mesh.shape["vox"], mesh.shape["scen"]
    placed = (P("scen", "vox", None, None), P("vox", None), P("vox"), P("vox"), P("vox"))
    return jax.shard_map(
        functools.partial(body, nv, ns),
        mesh=mesh, in_specs=placed, out_specs=(P("vox"), P("scen", "vox")), check_vma=False,
    )
```
